512 devices in a mesh: dp: 8 (over y, z_hi), rows: 64 (over z_lo, x, core).
Axes of the slice: x: 4, y: 4, z: 16 (z_hi: 2, z_lo: 8; z = z_hi * 8 + z_lo), core: 2. Of those that a mesh axis runs over, the one named last changes fastest.
Arguments:
- features: bfloat16 [8, 256, 256, 128], P('dp', 'rows'), may hold values from -6 to 6
- conv_weight: bfloat16 [3, 3, 128, 128], replicated, may hold values from -0.1875 to 0.1875
- out_weight: bfloat16 [128, 3], replicated, may hold values from -0.5 to 0.5
- targets: float32 [8, 256, 256, 3], P('dp', 'rows'), may hold values from -4 to 4
- disc_weight: float32 [3, 3, 3, 64], replicated, may hold values from -1.25 to 1.25
- disc_head: float32 [64], replicated, may hold values from -0.75 to 0.75
- lpips_weight: float32 [3, 3, 3, 64], replicated, may hold values from -1.25 to 1.25
- lpips_lin: float32 [64], replicated, may hold values from 0.1 to 1
Outputs:
- recon: float32 [8, 256, 256, 3], P('dp', 'rows')
- grad_features: bfloat16 [8, 256, 256, 128], P('dp', 'rows')
- grad_conv: float32 [3, 3, 128, 128], P(None, None, None, 'dp')
- grad_out: float32 [128, 3], P('dp')
The draws below stay inside these ranges and needn't reach their ends.
All inputs are finite; a program needn't handle non-finite values.
Results may differ from the reference program's by a relative error of at most 0.01.
Values may be sent and summed in bfloat16 or wider, within the bound.
No kernel may reach another device: no remote copies, remote signals or barrier semaphores. Data moves between devices by JAX's collectives and lax.ppermute only.
A program may use at most 64 MiB of HBM per device.

```python
import math
import jax
import jax.numpy as jnp
from jax import lax

CH = 128
DISC_CH = 64
PERC_CH = 64
COLS = 256
FRAMES = 1
HEIGHT = 256
ALL_FRAMES = 8
N_DP = 8


def block_scale(key, extent, split, smallest, top_value):
    level, own = 1.0, jax.random.fold_in(key, 6)
    for dim, blocks in split:
        draws = jnp.exp(jax.random.uniform(jax.random.fold_in(own, dim), (blocks,), jnp.float32, smallest / len(split), top_value / len(split)))
        level = level * jnp.repeat(draws, extent[dim] // blocks).reshape([-1 if axis == dim else 1 for axis in range(len(extent))])
    return level


def normal_values(stream_key, dims, scale, most, split=(), dtype=jnp.bfloat16):
    gain = block_scale(stream_key, dims, split, -0.22, 0.18) if split else 1.0
    array = jax.random.normal(stream_key, dims, jnp.float32) * scale * gain
    return jnp.minimum(jnp.maximum(array, -most), most).astype(dtype)


def setup_inputs(seed: int = 0) -> dict:
    arg_keys = jax.random.split(jax.random.key(seed), 9)
    return {
        "features": normal_values(arg_keys[0], (ALL_FRAMES, HEIGHT, COLS, CH), 1.0, 6.0, ((0, 8), (1, 64))),
        "conv_weight": normal_values(arg_keys[1], (3, 3, CH, CH), (9 * CH) ** -0.5, 0.1875),
        "out_weight": normal_values(arg_keys[2], (CH, 3), CH ** -0.5, 0.5),
        "targets": normal_values(arg_keys[3], (ALL_FRAMES, HEIGHT, COLS, 3), 0.6, 4.0, ((0, 8), (1, 64)), jnp.float32),
        "disc_weight": normal_values(arg_keys[4], (3, 3, 3, DISC_CH), 27 ** -0.5, 1.25, (), jnp.float32),
        "disc_head": normal_values(arg_keys[5], (DISC_CH,), DISC_CH ** -0.5, 0.75, (), jnp.float32),
        "lpips_weight": normal_values(arg_keys[6], (3, 3, 3, PERC_CH), 27 ** -0.5, 1.25, (), jnp.float32),
        "lpips_lin": jnp.clip(jnp.exp(jax.random.uniform(arg_keys[7], (PERC_CH,), jnp.float32, math.log(0.1), math.log(1.0))), 0.1, 1.0),
    }


adv_scale = 0.5
charb_eps = 0.01

def convolve(inputs, kernel, padding, precision):
    return lax.conv_general_dilated(inputs, kernel, (1, 1), padding, dimension_numbers=('NHWC', 'HWIO', 'NHWC'), preferred_element_type=jnp.float32, precision=precision)

def leaky_smooth(values):
    return 0.2 * values + 0.8 * jax.nn.softplus(values)

def loss_total(images, truth, disc_weight, disc_head, lpips_weight, lpips_lin, divisor):
    high = lax.Precision.HIGHEST
    same = ((1, 1), (1, 1))
    differ_img = images - truth
    recon_term = jnp.sum(jnp.sqrt(differ_img * differ_img + charb_eps))
    disc = leaky_smooth(convolve(images, disc_weight, same, high))
    logits = jnp.einsum('nhwc,c->nhw', disc, disc_head, precision=high)
    feats_a = jax.nn.gelu(convolve(images, lpips_weight, same, high), approximate=True)
    feats_b = jax.nn.gelu(convolve(truth, lpips_weight, same, high), approximate=True)
    norm_a = feats_a * lax.rsqrt(lax.optimization_barrier(jnp.mean(feats_a * feats_a, axis=-1, keepdims=True)) + 1e-06)
    norm_b = feats_b * lax.rsqrt(lax.optimization_barrier(jnp.mean(feats_b * feats_b, axis=-1, keepdims=True)) + 1e-06)
    differ = norm_a - norm_b
    percep = jnp.sum(differ * differ * lpips_lin)
    return (recon_term - adv_scale * jnp.sum(logits) + percep) / divisor

def weight_taps(padded, grad_pre, rows_loc, cols_loc):
    width = grad_pre.shape[-1]
    flat_grad = grad_pre.reshape(-1, width)
    result = []
    for row_tap in range(3):
        line = []
        for col_tap in range(3):
            window = padded[:, row_tap:row_tap + rows_loc, col_tap:col_tap + cols_loc, :].reshape(-1, padded.shape[-1])
            line.append(lax.dot_general(window, flat_grad, (((0,), (0,)), ((), ())), preferred_element_type=jnp.float32))
        result.append(jnp.stack(line))
    return jnp.stack(result)

def one_clip(features, truth, conv_weight, out_weight, disc_weight, disc_head, lpips_weight, lpips_lin):
    high = lax.Precision.HIGHEST
    frames, height, cols, width = features.shape
    preact = convolve(features, conv_weight, ((1, 1), (1, 1)), None)
    hidden = jax.nn.silu(preact).astype(jnp.bfloat16)
    recon = jnp.dot(hidden.reshape(-1, width), out_weight, preferred_element_type=jnp.float32).reshape(frames, height, cols, 3)
    grad_image = jax.grad(loss_total)(recon, truth, disc_weight, disc_head, lpips_weight, lpips_lin, frames)
    flat_img = grad_image.reshape(-1, 3)
    grad_hidden = jnp.dot(flat_img, out_weight.astype(jnp.float32).T, precision=high).reshape(preact.shape)
    sigma = jax.nn.sigmoid(preact)
    grad_pre = (grad_hidden * sigma * (1.0 + preact * (1.0 - sigma))).astype(jnp.bfloat16)
    flipped = jnp.transpose(conv_weight[::-1, ::-1], (0, 1, 3, 2))
    grad_features = convolve(grad_pre, flipped, ((1, 1), (1, 1)), None).astype(jnp.bfloat16)
    padded = jnp.pad(features, ((0, 0), (1, 1), (1, 1), (0, 0)))
    grad_conv = weight_taps(padded, grad_pre, height, cols)
    grad_out = jnp.dot(hidden.reshape(-1, width).astype(jnp.float32).T, flat_img, precision=high)
    return (recon, grad_features, grad_conv, grad_out)

def reference(features, conv_weight, out_weight, targets, disc_weight, disc_head, lpips_weight, lpips_lin):
    clips = features.reshape(N_DP, FRAMES, HEIGHT, COLS, CH)
    truths = targets.reshape(N_DP, FRAMES, HEIGHT, COLS, 3)

    def run(pair):
        return one_clip(pair[0], pair[1], conv_weight, out_weight, disc_weight, disc_head, lpips_weight, lpips_lin)
    recon, grad_features, grad_conv, grad_out = lax.map(run, (clips, truths))
    return (recon.reshape(ALL_FRAMES, HEIGHT, COLS, 3), grad_features.reshape(ALL_FRAMES, HEIGHT, COLS, CH), lax.optimization_barrier(jnp.sum(grad_conv, axis=0)), lax.optimization_barrier(jnp.sum(grad_out, axis=0)))
```

```python
import functools

import jax
import jax.numpy as jnp
import numpy as np
from jax import lax
from jax.experimental import pallas as pl
from jax.experimental.pallas import tpu as pltpu
from jax.sharding import Mesh, PartitionSpec as P

ADV_SCALE = 0.5
CHARB_EPS = 0.01
NORM_EPS = 1e-06
GELU_K = 0.7978845608028654
GELU_C = 0.044715

ROWS_LOC = 4
COLS = 256
CH = 128
TILES = 64
HEIGHT = ROWS_LOC * TILES
N_PRE = 10
N_LOSS = 8
N_GRAD = 6
PITCH = COLS + 8
K_BAND = 256
BLOCK = 20
PADDED = 24
VMEM = pltpu.VMEM


def band_selectors():
    ahead = np.zeros((32, N_LOSS * K_BAND), np.float32)
    back = np.zeros((N_LOSS * 3 * N_GRAD * 8, 32), np.float32)
    for a in range(3):
        for b in range(3):
            for c in range(3):
                tap = (a * 3 + b) * 3 + c
                for r in range(N_LOSS):
                    ahead[tap, r * K_BAND + b * N_PRE * 8 + (r + a) * 8 + c] = 1.0
                    q = r + a - 2
                    if 0 <= q < N_GRAD:
                        back[r * 3 * N_GRAD * 8 + b * N_GRAD * 8 + q * 8 + c, tap] = 1.0
    return ahead, back


def dot(a, b, ca, cb):
    return lax.dot_general(a, b, (((ca,), (cb,)), ((), ())), preferred_element_type=jnp.float32)


def sigmoid(x):
    return 0.5 * jnp.tanh(0.5 * x) + 0.5


def shifted(x, by):
    lane = lax.broadcasted_iota(jnp.int32, x.shape, 1)
    if by == 1:
        return jnp.where(lane == 0, 0.0, pltpu.roll(x, 1, 1))
    return jnp.where(lane == COLS - 1, 0.0, pltpu.roll(x, COLS - 1, 1))


def prep_kernel(w27_ref, ahead_ref, back_ref, band_ref, band_t_ref):
    w27 = w27_ref[...].astype(jnp.bfloat16)
    size = 3 * N_GRAD * 8
    for r in range(N_LOSS):
        band = dot(w27, ahead_ref[:, r * K_BAND : (r + 1) * K_BAND], 0, 0)
        band_ref[r * CH : (r + 1) * CH, :] = band.astype(jnp.bfloat16)
        back = dot(back_ref[r * size : (r + 1) * size, :], w27, 1, 0)
        band_t_ref[:, r * CH : (r + 1) * CH] = back.astype(jnp.bfloat16)


def main_kernel(
    tile_ref, up_ref, own_ref, down_ref, t_up_ref, t_own_ref, t_down_ref, conv_ref, out_w_ref,
    band_ref, band_t_ref, heads_ref,
    recon_ref, grad_pre_ref, piece_ref,
    y0, y1, y2, slope, hidden, truth, dall, packed,
):
    bf16, f32 = jnp.bfloat16, jnp.float32
    first_row = tile_ref[0] * ROWS_LOC

    def valid(row):
        inside = jnp.logical_and(first_row + row >= 0, first_row + row < HEIGHT)
        return jnp.where(inside, 1.0, 0.0).astype(f32)

    def feats(j):
        return (up_ref, own_ref, down_ref)[j // ROWS_LOC][j % ROWS_LOC]

    for buf in (y0, y2):
        for j in range(N_PRE + 1):
            buf[pl.ds(j * PITCH, 8), :] = jnp.zeros((8, CH), f32)
    weights = jnp.concatenate(
        [jnp.concatenate([conv_ref[a, b] for a in range(3)], axis=0) for b in range(3)], axis=1
    )
    out_w = out_w_ref[...]
    out_w16 = out_w.astype(bf16)
    image = []
    for j in range(N_PRE):
        lhs = jnp.concatenate([feats(j), feats(j + 1), feats(j + 2)], axis=1)
        prod = dot(lhs, weights, 1, 0)
        for b, buf in enumerate((y0, y1, y2)):
            buf[pl.ds(j * PITCH + 8, COLS), :] = prod[:, b * CH : (b + 1) * CH]
    for j in range(N_PRE):
        at = j * PITCH + 8
        pre = y0[pl.ds(at - 1, COLS), :] + y1[pl.ds(at, COLS), :] + y2[pl.ds(at + 1, COLS), :]
        sig = sigmoid(pre)
        act = (pre * sig).astype(bf16)
        if 2 <= j < 2 + N_GRAD:
            slope[j - 2] = sig * (1.0 + pre * (1.0 - sig))
        if 3 <= j < 3 + ROWS_LOC:
            hidden[j - 3] = act
        image.append(dot(out_w16, act, 1, 1) * valid(j - 3))
    for j in range(ROWS_LOC):
        for c in range(3):
            recon_ref[c, j : j + 1, :] = image[j + 3][c : c + 1, :]
    image = jnp.concatenate(image, axis=0)

    truth[...] = jnp.zeros_like(truth)
    for j in range(N_PRE):
        k = j + 1
        src = (t_up_ref, t_own_ref, t_down_ref)[k // ROWS_LOC]
        for c in range(3):
            truth[j * 8 + c : j * 8 + c + 1, :] = src[c, k % ROWS_LOC : k % ROWS_LOC + 1, :]
    true_image = truth[...]

    def taps(x):
        pad = jnp.zeros((K_BAND - 3 * N_PRE * 8, COLS), f32)
        return jnp.concatenate([shifted(x, 1), x, shifted(x, -1), pad], axis=0).astype(bf16)

    taps_a, taps_b = taps(image), taps(true_image)
    half = CH // 2

    def gelu(x):
        sq = x * x
        th = jnp.tanh(GELU_K * x * (1.0 + GELU_C * sq))
        low = 0.5 * (1.0 + th)
        return x * low, low, th, sq

    for r in range(N_LOSS):
        ok = valid(r - 2)
        both = dot(band_ref[r * CH : (r + 1) * CH, :], taps_a, 1, 0)
        other = dot(band_ref[r * CH + half : (r + 1) * CH, :], taps_b, 1, 0)
        for side in range(2):
            cols = slice(side * CH, (side + 1) * CH)
            g, a, t = both[:half, cols], both[half:, cols], other[:, cols]
            d_disc = (heads_ref[:half, :] * ok) * (0.2 + 0.8 * sigmoid(g))
            fa, low, th, sq = gelu(a)
            fb = gelu(t)[0]
            inv_a = lax.rsqrt(jnp.sum(fa * fa, axis=0, keepdims=True) * (1.0 / half) + NORM_EPS)
            inv_b = lax.rsqrt(jnp.sum(fb * fb, axis=0, keepdims=True) * (1.0 / half) + NORM_EPS)
            na = fa * inv_a
            up = (heads_ref[half:, :] * ok) * (na - fb * inv_b)
            mean = jnp.sum(up * na, axis=0, keepdims=True) * (1.0 / half)
            d_feat = inv_a * (up - na * mean)
            rise = low + 0.5 * a * (1.0 - th * th) * (GELU_K * (1.0 + 3.0 * GELU_C * sq))
            dall[r * CH : r * CH + half, cols] = d_disc.astype(bf16)
            dall[r * CH + half : (r + 1) * CH, cols] = (d_feat * rise).astype(bf16)

    back = dot(band_t_ref[...], dall[...], 1, 0)
    n = N_GRAD * 8
    diff = (image - true_image)[16 : 16 + n]
    grad_image = (
        shifted(back[:n], -1) + back[n : 2 * n] + shifted(back[2 * n :], 1)
        + diff * lax.rsqrt(diff * diff + CHARB_EPS)
    )
    out_w2 = jnp.concatenate([out_w, out_w], axis=0).astype(bf16)
    grad_out = jnp.zeros((16, CH), f32)
    for q in range(N_GRAD):
        g = grad_image[q * 8 : (q + 1) * 8] * valid(q - 1)
        high = g.astype(bf16).astype(f32)
        pair = jnp.concatenate([high, g - high], axis=0)
        grad_pre = dot(pair.T.astype(bf16), out_w2, 1, 0) * slope[q]
        grad_pre_ref[q] = grad_pre.astype(bf16)
        if 1 <= q <= ROWS_LOC:
            y0[pl.ds((q - 1) * PITCH + 8, COLS), :] = grad_pre
            grad_out = grad_out + dot(pair.astype(bf16), hidden[q - 1], 1, 0)
    grad_out = grad_out[:8] + grad_out[8:]

    lhs, rhs = [], []
    for y in range(ROWS_LOC):
        at = y * PITCH + 8
        lhs.append(
            jnp.concatenate([y0[pl.ds(at + 1 - b, COLS), :] for b in range(3)], axis=1).astype(bf16)
        )
        rhs.append(jnp.concatenate([feats(3 + y + a) for a in range(3)], axis=1))
    lhs, rhs = jnp.concatenate(lhs, axis=0), jnp.concatenate(rhs, axis=0)
    packed[...] = jnp.zeros_like(packed)
    for b in range(3):
        grad = dot(lhs[:, b * CH : (b + 1) * CH], rhs, 0, 0)
        for a in range(3):
            tap = a * 3 + b
            for d in range(8):
                block = grad[d * 16 : (d + 1) * 16, a * CH : (a + 1) * CH]
                start = tap * 16
                while start < tap * 16 + 16:
                    part, inner = divmod(start, 18)
                    count = min(18 - inner, tap * 16 + 16 - start)
                    at = ((d // 2) * 8 + part) * 2 * BLOCK + (d % 2) * BLOCK + inner
                    packed[pl.ds(at, count), :] = block[start - tap * 16 : start - tap * 16 + count]
                    start += count
    for d in range(8):
        for c in range(3):
            line = grad_out[c : c + 1]
            if d:
                line = pltpu.roll(line, CH - 16 * d, 1)
            packed[pl.ds(((d // 2) * 8 + c) * 2 * BLOCK + (d % 2) * BLOCK + 18, 1), :] = line
    piece_ref[...] = packed[...].astype(bf16)


def back_kernel(grad_ref, conv_ref, out_ref, z0, z1, z2):
    bf16, f32 = jnp.bfloat16, jnp.float32
    for buf in (z0, z2):
        for y in range(ROWS_LOC + 1):
            buf[pl.ds(y * PITCH, 8), :] = jnp.zeros((8, CH), f32)
    weights = jnp.concatenate(
        [jnp.concatenate([conv_ref[a, b] for a in range(3)], axis=1) for b in range(3)], axis=0
    )
    for y in range(ROWS_LOC):
        lhs = jnp.concatenate([grad_ref[y + 2 - a] for a in range(3)], axis=1)
        prod = dot(lhs, weights, 1, 1)
        for b, buf in enumerate((z0, z1, z2)):
            buf[pl.ds(y * PITCH + 8, COLS), :] = prod[:, b * CH : (b + 1) * CH]
    for y in range(ROWS_LOC):
        at = y * PITCH + 8
        total = z0[pl.ds(at + 1, COLS), :] + z1[pl.ds(at, COLS), :] + z2[pl.ds(at - 1, COLS), :]
        out_ref[y] = total.astype(bf16)


def first_sum_kernel(in_ref, out_ref):
    total = in_ref[0].astype(jnp.float32)
    for k in range(1, in_ref.shape[0]):
        total = total + in_ref[k].astype(jnp.float32)
    pad = jnp.zeros((PADDED - BLOCK, CH), jnp.float32)
    for half in range(2):
        part = jnp.concatenate([total[half * BLOCK : (half + 1) * BLOCK], pad], axis=0)
        for k in range(8):
            out_ref[half * 8 + k] = part.astype(jnp.bfloat16)


def second_sum_kernel(in_ref, out_ref):
    total = in_ref[0].astype(jnp.float32)
    for k in range(1, in_ref.shape[0]):
        total = total + in_ref[k].astype(jnp.float32)
    for k in range(8):
        out_ref[k] = total


def last_kernel(in_ref, conv_ref, out_ref):
    for k in range(8):
        conv_ref[pl.ds(k * 18, 18), :] = in_ref[k, 0:18, :]
    for c in range(3):
        out_ref[c : c + 1, :] = in_ref[c, 18:19, :16]


def call(kernel, out_shape, scratch=(), smem=0, n_in=1, flops=0, name=None):
    specs = [pl.BlockSpec(memory_space=pltpu.SMEM)] * smem
    specs += [pl.BlockSpec(memory_space=VMEM)] * (n_in - smem)
    many = isinstance(out_shape, tuple)
    return pl.pallas_call(
        kernel,
        out_shape=out_shape,
        in_specs=specs,
        out_specs=tuple(pl.BlockSpec(memory_space=VMEM) for _ in out_shape)
        if many
        else pl.BlockSpec(memory_space=VMEM),
        scratch_shapes=list(scratch),
        cost_estimate=pl.CostEstimate(flops=flops, bytes_accessed=1 << 20, transcendentals=0),
        name=name,
    )


def shape(*dims, dtype=jnp.float32):
    return jax.ShapeDtypeStruct(dims, dtype)


def prepare(disc_weight, disc_head, lpips_weight, lpips_lin, out_weight):
    f32 = jnp.float32
    ahead, back = band_selectors()
    w27 = jnp.concatenate([disc_weight.reshape(27, 64), lpips_weight.reshape(27, 64)], axis=1)
    w27 = jnp.pad(w27, ((0, 5), (0, 0)))
    heads = jnp.concatenate([-ADV_SCALE * disc_head, 2.0 * lpips_lin])
    heads = jnp.broadcast_to(heads[:, None], (128, 128))
    out_w = jnp.pad(out_weight.astype(f32).T, ((0, 5), (0, 0)))
    band, band_t = call(
        prep_kernel,
        (
            shape(N_LOSS * CH, K_BAND, dtype=jnp.bfloat16),
            shape(3 * N_GRAD * 8, N_LOSS * CH, dtype=jnp.bfloat16),
        ),
        n_in=3,
        flops=1 << 28,
        name="bands",
    )(w27, jnp.asarray(ahead, jnp.bfloat16), jnp.asarray(back, jnp.bfloat16))
    return band, band_t, heads, out_w


def tile_step(tile, up, own, down, t_up, t_own, t_down, conv_weight, out_w, band, band_t, heads):
    f32, bf16 = jnp.float32, jnp.bfloat16
    rows = N_PRE * PITCH + 8
    return call(
        main_kernel,
        (
            shape(3, ROWS_LOC, COLS),
            shape(N_GRAD, COLS, CH, dtype=bf16),
            shape(32 * 2 * BLOCK, CH, dtype=bf16),
        ),
        scratch=[
            VMEM((rows, CH), f32),
            VMEM((rows, CH), f32),
            VMEM((rows, CH), f32),
            VMEM((N_GRAD, COLS, CH), f32),
            VMEM((ROWS_LOC, COLS, CH), bf16),
            VMEM((N_PRE * 8, COLS), f32),
            VMEM((N_LOSS * CH, COLS), bf16),
            VMEM((32 * 2 * BLOCK, CH), f32),
        ],
        smem=1,
        n_in=12,
        flops=1 << 31,
        name="tile",
    )(tile, up, own, down, t_up, t_own, t_down, conv_weight, out_w, band, band_t, heads)


def back_step(grad_pre, conv_weight):
    rows = ROWS_LOC * PITCH + 8
    return call(
        back_kernel,
        shape(ROWS_LOC, COLS, CH, dtype=jnp.bfloat16),
        scratch=[VMEM((rows, CH), jnp.float32)] * 3,
        n_in=2,
        flops=1 << 30,
        name="features_back",
    )(grad_pre, conv_weight)


def swap(array, axes):
    return lax.all_to_all(array, axes, split_axis=0, concat_axis=0, tiled=True)


ROWS = ("zl", "x", "core")


def body(
    features, conv_weight, out_weight, targets, disc_weight, disc_head, lpips_weight, lpips_lin
):
    own = features[0]
    t_own = jnp.transpose(targets[0], (2, 0, 1))
    fall = [(i, i + 1) for i in range(TILES - 1)]
    rise = [(i + 1, i) for i in range(TILES - 1)]
    up, down = lax.ppermute(own, ROWS, fall), lax.ppermute(own, ROWS, rise)
    t_up, t_down = lax.ppermute(t_own, ROWS, fall), lax.ppermute(t_own, ROWS, rise)
    band, band_t, heads, out_w = prepare(
        disc_weight, disc_head, lpips_weight, lpips_lin, out_weight
    )
    tile = lax.axis_index(ROWS).astype(jnp.int32).reshape(1)
    recon, grad_pre, pieces = tile_step(
        tile, up, own, down, t_up, t_own, t_down, conv_weight, out_w, band, band_t, heads
    )
    grad_features = back_step(grad_pre, conv_weight)
    pieces = swap(pieces.reshape(32, 2 * BLOCK, CH), ("y", "x", "core"))
    pieces = call(first_sum_kernel, shape(16, PADDED, CH, dtype=jnp.bfloat16), name="sum_1")(pieces)
    pieces = swap(pieces, ("zh", "zl"))
    pieces = call(second_sum_kernel, shape(8, PADDED, CH), name="sum_2")(pieces)
    pieces = swap(pieces, ("x", "core"))
    grad_conv, grad_out = call(last_kernel, (shape(144, CH), shape(3, 16)), name="join")(pieces)
    return (
        jnp.transpose(recon, (1, 2, 0))[None],
        grad_features[None],
        jnp.transpose(grad_conv.reshape(3, 3, 16, CH), (0, 1, 3, 2)),
        grad_out.T,
    )


def solution(mesh):
    fine = Mesh(mesh.devices.reshape(4, 2, 8, 4, 2), ("y", "zh", "zl", "x", "core"))
    dp = ("y", "zh")
    in_specs = (
        P(dp, ROWS, None, None), P(), P(), P(dp, ROWS, None, None), P(), P(), P(), P(),
    )
    out_specs = (
        P(dp, ROWS, None, None), P(dp, ROWS, None, None), P(None, None, None, dp), P(dp, None),
    )
    return jax.shard_map(body, mesh=fine, in_specs=in_specs, out_specs=out_specs, check_vma=False)
```

```python
import functools

import jax
import jax.numpy as jnp
import numpy as np
from jax import lax
from jax.experimental import pallas as pl
from jax.experimental.pallas import tpu as pltpu
from jax.sharding import Mesh, PartitionSpec as P

ADV_SCALE = 0.5
CHARB_EPS = 0.01
NORM_EPS = 1e-06
GELU_K = 0.7978845608028654
GELU_C = 0.044715

ROWS_LOC = 4
COLS = 256
TILE = ROWS_LOC * COLS
CH = 128
TILES = 64
HEIGHT = ROWS_LOC * TILES
N_PRE = 10
N_LOSS = 8
N_GRAD = 6
PITCH = COLS + 8
K_BAND = 256
BLOCK = 20
PADDED = 24
VMEM = pltpu.VMEM


def band_selectors():
    ahead = np.zeros((32, N_LOSS * K_BAND), np.float32)
    back = np.zeros((N_LOSS * 3 * N_GRAD * 8, 32), np.float32)
    for a in range(3):
        for b in range(3):
            for c in range(3):
                tap = (a * 3 + b) * 3 + c
                for r in range(N_LOSS):
                    ahead[tap, r * K_BAND + b * N_PRE * 8 + (r + a) * 8 + c] = 1.0
                    q = r + a - 2
                    if 0 <= q < N_GRAD:
                        back[r * 3 * N_GRAD * 8 + b * N_GRAD * 8 + q * 8 + c, tap] = 1.0
    return ahead, back


def dot(a, b, ca, cb):
    return lax.dot_general(a, b, (((ca,), (cb,)), ((), ())), preferred_element_type=jnp.float32)


def sigmoid(x):
    return 0.5 * jnp.tanh(0.5 * x) + 0.5


def shifted(x, by):
    lane = lax.broadcasted_iota(jnp.int32, x.shape, 1)
    if by == 1:
        return jnp.where(lane == 0, 0.0, pltpu.roll(x, 1, 1))
    return jnp.where(lane == COLS - 1, 0.0, pltpu.roll(x, COLS - 1, 1))


def pack_kernel(own_ref, truth_ref, out_ref, sem):
    copy = pltpu.make_async_copy(own_ref, out_ref.at[pl.ds(0, TILE)], sem)
    copy.start()
    rows = [
        truth_ref[c, :, h * CH : (h + 1) * CH] for c in range(3) for h in range(COLS // CH)
    ] + [jnp.zeros((8, CH), jnp.float32)]
    exact = jnp.concatenate(rows, axis=0)
    high = exact.astype(jnp.bfloat16)
    out_ref[pl.ds(TILE, 32), :] = high
    out_ref[pl.ds(TILE + 32, 32), :] = (exact - high.astype(jnp.float32)).astype(jnp.bfloat16)
    copy.wait()


def prep_kernel(
    disc_ref, lpips_ref, head_ref, lin_ref, out_w_ref, ahead_ref, back_ref,
    band_ref, band_t_ref, heads_ref, wide_ref, w27_ref,
):
    w27_ref[...] = jnp.zeros_like(w27_ref)
    for a in range(3):
        for b in range(3):
            pair = jnp.concatenate([disc_ref[a, b], lpips_ref[a, b]], axis=1)
            w27_ref[pl.ds((a * 3 + b) * 3, 3), :] = pair
    w27 = w27_ref[...].astype(jnp.bfloat16)
    size = 3 * N_GRAD * 8
    for r in range(N_LOSS):
        band = dot(w27, ahead_ref[:, r * K_BAND : (r + 1) * K_BAND], 0, 0)
        band_ref[r * CH : (r + 1) * CH, :] = band.astype(jnp.bfloat16)
        back = dot(back_ref[r * size : (r + 1) * size, :], w27, 1, 0)
        band_t_ref[:, r * CH : (r + 1) * CH] = back.astype(jnp.bfloat16)
    line = jnp.concatenate([-ADV_SCALE * head_ref[...], 2.0 * lin_ref[...]], axis=1)
    heads_ref[...] = jnp.broadcast_to(line, (CH, CH)).T
    wide_ref[...] = jnp.zeros_like(wide_ref)
    wide_ref[0:3, :] = out_w_ref[...].astype(jnp.float32)


def main_kernel(
    tile_ref, up_ref, own_ref, down_ref, conv_ref, out_w_ref,
    band_ref, band_t_ref, heads_ref,
    recon_ref, grad_pre_ref, piece_ref,
    y0, y1, y2, slope, hidden, truth, dall, packed,
):
    bf16, f32 = jnp.bfloat16, jnp.float32
    first_row = tile_ref[0] * ROWS_LOC

    def valid(row):
        inside = jnp.logical_and(first_row + row >= 0, first_row + row < HEIGHT)
        return jnp.where(inside, 1.0, 0.0).astype(f32)

    def feats(j):
        return (up_ref, own_ref, down_ref)[j // ROWS_LOC][pl.ds(j % ROWS_LOC * COLS, COLS), :]

    for buf in (y0, y2):
        for j in range(N_PRE + 1):
            buf[pl.ds(j * PITCH, 8), :] = jnp.zeros((8, CH), f32)
    weights = jnp.concatenate(
        [jnp.concatenate([conv_ref[a, b] for a in range(3)], axis=0) for b in range(3)], axis=1
    )
    out_w = out_w_ref[...]
    out_w16 = out_w.astype(bf16)
    image = []
    for j in range(N_PRE):
        lhs = jnp.concatenate([feats(j), feats(j + 1), feats(j + 2)], axis=1)
        prod = dot(lhs, weights, 1, 0)
        for b, buf in enumerate((y0, y1, y2)):
            buf[pl.ds(j * PITCH + 8, COLS), :] = prod[:, b * CH : (b + 1) * CH]
    for j in range(N_PRE):
        at = j * PITCH + 8
        pre = y0[pl.ds(at - 1, COLS), :] + y1[pl.ds(at, COLS), :] + y2[pl.ds(at + 1, COLS), :]
        sig = sigmoid(pre)
        act = (pre * sig).astype(bf16)
        if 2 <= j < 2 + N_GRAD:
            slope[j - 2] = sig * (1.0 + pre * (1.0 - sig))
        if 3 <= j < 3 + ROWS_LOC:
            hidden[j - 3] = act
        image.append(dot(out_w16, act, 1, 1) * valid(j - 3))
    for j in range(ROWS_LOC):
        for c in range(3):
            recon_ref[c, j : j + 1, :] = image[j + 3][c : c + 1, :]
    image = jnp.concatenate(image, axis=0)

    truth[...] = jnp.zeros_like(truth)
    targets = [
        ref[pl.ds(TILE, 32), :].astype(f32) + ref[pl.ds(TILE + 32, 32), :].astype(f32)
        for ref in (up_ref, own_ref, down_ref)
    ]
    for j in range(N_PRE):
        src, row = targets[(j + 1) // ROWS_LOC], (j + 1) % ROWS_LOC
        for c in range(3):
            for h in range(COLS // CH):
                at = (c * 2 + h) * ROWS_LOC + row
                truth[j * 8 + c : j * 8 + c + 1, h * CH : (h + 1) * CH] = src[at : at + 1]
    true_image = truth[...]

    def taps(x):
        pad = jnp.zeros((K_BAND - 3 * N_PRE * 8, COLS), f32)
        return jnp.concatenate([shifted(x, 1), x, shifted(x, -1), pad], axis=0).astype(bf16)

    taps_a, taps_b = taps(image), taps(true_image)
    half = CH // 2

    def gelu(x):
        sq = x * x
        th = jnp.tanh(GELU_K * x * (1.0 + GELU_C * sq))
        low = 0.5 * (1.0 + th)
        return x * low, low, th, sq

    for r in range(N_LOSS):
        ok = valid(r - 2)
        both = dot(band_ref[r * CH : (r + 1) * CH, :], taps_a, 1, 0)
        other = dot(band_ref[r * CH + half : (r + 1) * CH, :], taps_b, 1, 0)
        for side in range(2):
            cols = slice(side * CH, (side + 1) * CH)
            g, a, t = both[:half, cols], both[half:, cols], other[:, cols]
            d_disc = (heads_ref[:half, :] * ok) * (0.2 + 0.8 * sigmoid(g))
            fa, low, th, sq = gelu(a)
            fb = gelu(t)[0]
            inv_a = lax.rsqrt(jnp.sum(fa * fa, axis=0, keepdims=True) * (1.0 / half) + NORM_EPS)
            inv_b = lax.rsqrt(jnp.sum(fb * fb, axis=0, keepdims=True) * (1.0 / half) + NORM_EPS)
            na = fa * inv_a
            up = (heads_ref[half:, :] * ok) * (na - fb * inv_b)
            mean = jnp.sum(up * na, axis=0, keepdims=True) * (1.0 / half)
            d_feat = inv_a * (up - na * mean)
            rise = low + 0.5 * a * (1.0 - th * th) * (GELU_K * (1.0 + 3.0 * GELU_C * sq))
            dall[r * CH : r * CH + half, cols] = d_disc.astype(bf16)
            dall[r * CH + half : (r + 1) * CH, cols] = (d_feat * rise).astype(bf16)

    back = dot(band_t_ref[...], dall[...], 1, 0)
    n = N_GRAD * 8
    diff = (image - true_image)[16 : 16 + n]
    grad_image = (
        shifted(back[:n], -1) + back[n : 2 * n] + shifted(back[2 * n :], 1)
        + diff * lax.rsqrt(diff * diff + CHARB_EPS)
    )
    out_w2 = jnp.concatenate([out_w, out_w], axis=0).astype(bf16)
    grad_out = jnp.zeros((16, CH), f32)
    for q in range(N_GRAD):
        g = grad_image[q * 8 : (q + 1) * 8] * valid(q - 1)
        high = g.astype(bf16).astype(f32)
        pair = jnp.concatenate([high, g - high], axis=0)
        grad_pre = dot(pair.T.astype(bf16), out_w2, 1, 0) * slope[q]
        grad_pre_ref[q] = grad_pre.astype(bf16)
        if 1 <= q <= ROWS_LOC:
            y0[pl.ds((q - 1) * PITCH + 8, COLS), :] = grad_pre
            grad_out = grad_out + dot(pair.astype(bf16), hidden[q - 1], 1, 0)
    grad_out = grad_out[:8] + grad_out[8:]

    lhs, rhs = [], []
    for y in range(ROWS_LOC):
        at = y * PITCH + 8
        lhs.append(
            jnp.concatenate([y0[pl.ds(at + 1 - b, COLS), :] for b in range(3)], axis=1).astype(bf16)
        )
        rhs.append(jnp.concatenate([feats(3 + y + a) for a in range(3)], axis=1))
    lhs, rhs = jnp.concatenate(lhs, axis=0), jnp.concatenate(rhs, axis=0)
    packed[...] = jnp.zeros_like(packed)
    for b in range(3):
        grad = dot(lhs[:, b * CH : (b + 1) * CH], rhs, 0, 0)
        for a in range(3):
            tap = a * 3 + b
            for d in range(8):
                block = grad[d * 16 : (d + 1) * 16, a * CH : (a + 1) * CH]
                start = tap * 16
                while start < tap * 16 + 16:
                    part, inner = divmod(start, 18)
                    count = min(18 - inner, tap * 16 + 16 - start)
                    at = ((d // 2) * 8 + part) * 2 * BLOCK + (d % 2) * BLOCK + inner
                    packed[pl.ds(at, count), :] = block[start - tap * 16 : start - tap * 16 + count]
                    start += count
    for d in range(8):
        for c in range(3):
            line = grad_out[c : c + 1]
            if d:
                line = pltpu.roll(line, CH - 16 * d, 1)
            packed[pl.ds(((d // 2) * 8 + c) * 2 * BLOCK + (d % 2) * BLOCK + 18, 1), :] = line
    piece_ref[...] = packed[...].astype(bf16)


def back_kernel(grad_ref, conv_ref, out_ref, z0, z1, z2):
    bf16, f32 = jnp.bfloat16, jnp.float32
    for buf in (z0, z2):
        for y in range(ROWS_LOC + 1):
            buf[pl.ds(y * PITCH, 8), :] = jnp.zeros((8, CH), f32)
    weights = jnp.concatenate(
        [jnp.concatenate([conv_ref[a, b] for a in range(3)], axis=1) for b in range(3)], axis=0
    )
    for y in range(ROWS_LOC):
        lhs = jnp.concatenate([grad_ref[y + 2 - a] for a in range(3)], axis=1)
        prod = dot(lhs, weights, 1, 1)
        for b, buf in enumerate((z0, z1, z2)):
            buf[pl.ds(y * PITCH + 8, COLS), :] = prod[:, b * CH : (b + 1) * CH]
    for y in range(ROWS_LOC):
        at = y * PITCH + 8
        total = z0[pl.ds(at + 1, COLS), :] + z1[pl.ds(at, COLS), :] + z2[pl.ds(at - 1, COLS), :]
        out_ref[y] = total.astype(bf16)


def first_sum_kernel(in_ref, out_ref):
    total = in_ref[0].astype(jnp.float32)
    for k in range(1, in_ref.shape[0]):
        total = total + in_ref[k].astype(jnp.float32)
    pad = jnp.zeros((PADDED - BLOCK, CH), jnp.float32)
    for half in range(2):
        part = jnp.concatenate([total[half * BLOCK : (half + 1) * BLOCK], pad], axis=0)
        for k in range(8):
            out_ref[half * 8 + k] = part.astype(jnp.bfloat16)


def second_sum_kernel(in_ref, out_ref):
    total = in_ref[0].astype(jnp.float32)
    for k in range(1, in_ref.shape[0]):
        total = total + in_ref[k].astype(jnp.float32)
    for k in range(8):
        out_ref[k] = total


def last_kernel(in_ref, conv_ref, out_ref):
    for k in range(8):
        conv_ref[pl.ds(k * 18, 18), :] = in_ref[k, 0:18, :]
    for c in range(3):
        out_ref[c : c + 1, :] = in_ref[c, 18:19, :16]


def call(kernel, out_shape, scratch=(), smem=0, whole=0, n_in=1, flops=0, name=None, vmem=4):
    specs = [pl.BlockSpec(memory_space=pltpu.SMEM)] * smem
    specs += [pl.BlockSpec(memory_space=pl.ANY)] * whole
    specs += [pl.BlockSpec(memory_space=VMEM)] * (n_in - smem - whole)
    many = isinstance(out_shape, tuple)
    return pl.pallas_call(
        kernel,
        out_shape=out_shape,
        in_specs=specs,
        out_specs=tuple(pl.BlockSpec(memory_space=VMEM) for _ in out_shape)
        if many
        else pl.BlockSpec(memory_space=VMEM),
        scratch_shapes=list(scratch),
        cost_estimate=pl.CostEstimate(flops=flops, bytes_accessed=1 << 20, transcendentals=0),
        compiler_params=pltpu.CompilerParams(vmem_limit_bytes=vmem << 20),
        name=name,
    )


def shape(*dims, dtype=jnp.float32):
    return jax.ShapeDtypeStruct(dims, dtype)


def pack(features, targets):
    return call(
        pack_kernel,
        shape(TILE + 64, CH, dtype=jnp.bfloat16),
        scratch=[pltpu.SemaphoreType.DMA],
        n_in=2,
        whole=1,
        name="pack",
    )(features.reshape(TILE, CH), targets)


def prepare(disc_weight, disc_head, lpips_weight, lpips_lin, out_weight):
    bf16 = jnp.bfloat16
    ahead, back = band_selectors()
    return call(
        prep_kernel,
        (
            shape(N_LOSS * CH, K_BAND, dtype=bf16),
            shape(3 * N_GRAD * 8, N_LOSS * CH, dtype=bf16),
            shape(CH, CH),
            shape(8, CH),
        ),
        scratch=[VMEM((32, CH), jnp.float32)],
        n_in=7,
        flops=1 << 28,
        name="bands",
    )(
        disc_weight, lpips_weight, disc_head.reshape(1, -1), lpips_lin.reshape(1, -1),
        out_weight.T, jnp.asarray(ahead, bf16), jnp.asarray(back, bf16),
    )


def tile_step(tile, up, own, down, conv_weight, band, band_t, heads, out_w):
    f32, bf16 = jnp.float32, jnp.bfloat16
    rows = N_PRE * PITCH + 8
    return call(
        main_kernel,
        (
            shape(3, ROWS_LOC, COLS),
            shape(N_GRAD, COLS, CH, dtype=bf16),
            shape(32 * 2 * BLOCK, CH, dtype=bf16),
        ),
        scratch=[
            VMEM((rows, CH), f32),
            VMEM((rows, CH), f32),
            VMEM((rows, CH), f32),
            VMEM((N_GRAD, COLS, CH), f32),
            VMEM((ROWS_LOC, COLS, CH), bf16),
            VMEM((N_PRE * 8, COLS), f32),
            VMEM((N_LOSS * CH, COLS), bf16),
            VMEM((32 * 2 * BLOCK, CH), f32),
        ],
        smem=1,
        n_in=9,
        flops=1 << 31,
        name="tile",
        vmem=20,
    )(tile, up, own, down, conv_weight, out_w, band, band_t, heads)


def back_step(grad_pre, conv_weight):
    rows = ROWS_LOC * PITCH + 8
    return call(
        back_kernel,
        shape(ROWS_LOC, COLS, CH, dtype=jnp.bfloat16),
        scratch=[VMEM((rows, CH), jnp.float32)] * 3,
        n_in=2,
        flops=1 << 30,
        name="features_back",
        vmem=8,
    )(grad_pre, conv_weight)


def swap(array, axes):
    return lax.all_to_all(array, axes, split_axis=0, concat_axis=0, tiled=True)


ROWS = ("zl", "x", "core")


def body(
    features, conv_weight, out_weight, targets, disc_weight, disc_head, lpips_weight, lpips_lin
):
    own = pack(features[0], jnp.transpose(targets[0], (2, 0, 1)))
    up = lax.ppermute(own, ROWS, [(i, i + 1) for i in range(TILES - 1)])
    down = lax.ppermute(own, ROWS, [(i + 1, i) for i in range(TILES - 1)])
    tables = prepare(disc_weight, disc_head, lpips_weight, lpips_lin, out_weight)
    tile = lax.axis_index(ROWS).astype(jnp.int32).reshape(1)
    recon, grad_pre, pieces = tile_step(tile, up, own, down, conv_weight, *tables)
    grad_features = back_step(grad_pre, conv_weight)
    pieces = swap(pieces.reshape(32, 2 * BLOCK, CH), ("y", "x", "core"))
    pieces = call(first_sum_kernel, shape(16, PADDED, CH, dtype=jnp.bfloat16), name="sum_1")(pieces)
    pieces = swap(pieces, ("zh", "zl"))
    pieces = call(second_sum_kernel, shape(8, PADDED, CH), name="sum_2")(pieces)
    pieces = swap(pieces, ("x", "core"))
    grad_conv, grad_out = call(last_kernel, (shape(144, CH), shape(3, 16)), name="join")(pieces)
    return (
        jnp.transpose(recon, (1, 2, 0))[None],
        grad_features[None],
        jnp.transpose(grad_conv.reshape(3, 3, 16, CH), (0, 1, 3, 2)),
        grad_out.T,
    )


def solution(mesh):
    fine = Mesh(mesh.devices.reshape(4, 2, 8, 4, 2), ("y", "zh", "zl", "x", "core"))
    dp = ("y", "zh")
    in_specs = (
        P(dp, ROWS, None, None), P(), P(), P(dp, ROWS, None, None), P(), P(), P(), P(),
    )
    out_specs = (
        P(dp, ROWS, None, None), P(dp, ROWS, None, None), P(None, None, None, dp), P(dp, None),
    )
    return jax.shard_map(body, mesh=fine, in_specs=in_specs, out_specs=out_specs, check_vma=False)
```

```python
import functools

import jax
import jax.numpy as jnp
import numpy as np
from jax import lax
from jax.experimental import pallas as pl
from jax.experimental.pallas import tpu as pltpu
from jax.sharding import Mesh, PartitionSpec as P

ADV_SCALE = 0.5
CHARB_EPS = 0.01
NORM_EPS = 1e-06
GELU_K = 0.7978845608028654
GELU_C = 0.044715

ROWS_LOC = 4
COLS = 256
TILE = ROWS_LOC * COLS
CH = 128
TILES = 64
HEIGHT = ROWS_LOC * TILES
N_PRE = 10
N_LOSS = 8
N_GRAD = 6
PITCH = COLS + 8
K_BAND = 256
BLOCK = 20
PADDED = 24
VMEM = pltpu.VMEM


def band_selectors():
    ahead = np.zeros((32, N_LOSS * K_BAND), np.float32)
    back = np.zeros((N_LOSS * 3 * N_GRAD * 8, 32), np.float32)
    for a in range(3):
        for b in range(3):
            for c in range(3):
                tap = (a * 3 + b) * 3 + c
                for r in range(N_LOSS):
                    ahead[tap, r * K_BAND + b * N_PRE * 8 + (r + a) * 8 + c] = 1.0
                    q = r + a - 2
                    if 0 <= q < N_GRAD:
                        back[r * 3 * N_GRAD * 8 + b * N_GRAD * 8 + q * 8 + c, tap] = 1.0
    return ahead, back


def dot(a, b, ca, cb):
    return lax.dot_general(a, b, (((ca,), (cb,)), ((), ())), preferred_element_type=jnp.float32)


def sigmoid(x):
    return 0.5 * jnp.tanh(0.5 * x) + 0.5


def shifted(x, by):
    lane = lax.broadcasted_iota(jnp.int32, x.shape, 1)
    if by == 1:
        return jnp.where(lane == 0, 0.0, pltpu.roll(x, 1, 1))
    return jnp.where(lane == COLS - 1, 0.0, pltpu.roll(x, COLS - 1, 1))


def pack_kernel(own_ref, truth_ref, out_ref, truth_vmem, sems):
    copy = pltpu.make_async_copy(own_ref, out_ref.at[pl.ds(0, TILE)], sems.at[0])
    copy.start()
    fetch = pltpu.make_async_copy(truth_ref, truth_vmem, sems.at[1])
    fetch.start()
    fetch.wait()
    rows = [
        truth_vmem[c, :, h * CH : (h + 1) * CH] for c in range(3) for h in range(COLS // CH)
    ] + [jnp.zeros((8, CH), jnp.float32)]
    exact = jnp.concatenate(rows, axis=0)
    high = exact.astype(jnp.bfloat16)
    out_ref[pl.ds(TILE, 32), :] = high
    out_ref[pl.ds(TILE + 32, 32), :] = (exact - high.astype(jnp.float32)).astype(jnp.bfloat16)
    copy.wait()


def prep_kernel(
    disc_ref, lpips_ref, head_ref, lin_ref, out_w_ref, ahead_ref, back_ref,
    band_ref, band_t_ref, heads_ref, wide_ref, w27_ref,
):
    w27_ref[...] = jnp.zeros_like(w27_ref)
    for a in range(3):
        for b in range(3):
            pair = jnp.concatenate([disc_ref[a, b], lpips_ref[a, b]], axis=1)
            w27_ref[pl.ds((a * 3 + b) * 3, 3), :] = pair
    w27 = w27_ref[...].astype(jnp.bfloat16)
    size = 3 * N_GRAD * 8
    for r in range(N_LOSS):
        band = dot(w27, ahead_ref[:, r * K_BAND : (r + 1) * K_BAND], 0, 0)
        band_ref[r * CH : (r + 1) * CH, :] = band.astype(jnp.bfloat16)
        back = dot(back_ref[r * size : (r + 1) * size, :], w27, 1, 0)
        band_t_ref[:, r * CH : (r + 1) * CH] = back.astype(jnp.bfloat16)
    line = jnp.concatenate([-ADV_SCALE * head_ref[...], 2.0 * lin_ref[...]], axis=1)
    heads_ref[...] = jnp.broadcast_to(line, (CH, CH)).T
    wide_ref[...] = jnp.zeros_like(wide_ref)
    wide_ref[0:3, :] = out_w_ref[...].astype(jnp.float32)


def main_kernel(
    tile_ref, near_ref, own_ref, far_ref, conv_ref, out_w_ref,
    band_ref, band_t_ref, heads_ref,
    recon_ref, grad_pre_ref, piece_ref,
    y0, y1, y2, slope, hidden, truth, dall, packed, up_ref, down_ref,
):
    bf16, f32 = jnp.bfloat16, jnp.float32

    @pl.when(lax.rem(tile_ref[0], 2) == 0)
    def _():
        up_ref[...] = far_ref[...]
        down_ref[...] = near_ref[...]

    @pl.when(lax.rem(tile_ref[0], 2) == 1)
    def _():
        up_ref[...] = near_ref[...]
        down_ref[...] = far_ref[...]

    first_row = tile_ref[0] * ROWS_LOC

    def valid(row):
        inside = jnp.logical_and(first_row + row >= 0, first_row + row < HEIGHT)
        return jnp.where(inside, 1.0, 0.0).astype(f32)

    def feats(j):
        return (up_ref, own_ref, down_ref)[j // ROWS_LOC][pl.ds(j % ROWS_LOC * COLS, COLS), :]

    for buf in (y0, y2):
        for j in range(N_PRE + 1):
            buf[pl.ds(j * PITCH, 8), :] = jnp.zeros((8, CH), f32)
    weights = jnp.concatenate(
        [jnp.concatenate([conv_ref[a, b] for a in range(3)], axis=0) for b in range(3)], axis=1
    )
    out_w = out_w_ref[...]
    out_w16 = out_w.astype(bf16)
    image = []
    for j in range(N_PRE):
        lhs = jnp.concatenate([feats(j), feats(j + 1), feats(j + 2)], axis=1)
        prod = dot(lhs, weights, 1, 0)
        for b, buf in enumerate((y0, y1, y2)):
            buf[pl.ds(j * PITCH + 8, COLS), :] = prod[:, b * CH : (b + 1) * CH]
    for j in range(N_PRE):
        at = j * PITCH + 8
        pre = y0[pl.ds(at - 1, COLS), :] + y1[pl.ds(at, COLS), :] + y2[pl.ds(at + 1, COLS), :]
        sig = sigmoid(pre)
        act = (pre * sig).astype(bf16)
        if 2 <= j < 2 + N_GRAD:
            slope[j - 2] = sig * (1.0 + pre * (1.0 - sig))
        if 3 <= j < 3 + ROWS_LOC:
            hidden[j - 3] = act
        image.append(dot(out_w16, act, 1, 1) * valid(j - 3))
    for j in range(ROWS_LOC):
        for c in range(3):
            recon_ref[c, j : j + 1, :] = image[j + 3][c : c + 1, :]
    image = jnp.concatenate(image, axis=0)

    truth[...] = jnp.zeros_like(truth)
    targets = [
        ref[pl.ds(TILE, 32), :].astype(f32) + ref[pl.ds(TILE + 32, 32), :].astype(f32)
        for ref in (up_ref, own_ref, down_ref)
    ]
    for j in range(N_PRE):
        src, row = targets[(j + 1) // ROWS_LOC], (j + 1) % ROWS_LOC
        for c in range(3):
            for h in range(COLS // CH):
                at = (c * 2 + h) * ROWS_LOC + row
                truth[j * 8 + c : j * 8 + c + 1, h * CH : (h + 1) * CH] = src[at : at + 1]
    true_image = truth[...]

    def taps(x):
        pad = jnp.zeros((K_BAND - 3 * N_PRE * 8, COLS), f32)
        return jnp.concatenate([shifted(x, 1), x, shifted(x, -1), pad], axis=0).astype(bf16)

    taps_a, taps_b = taps(image), taps(true_image)
    half = CH // 2

    def gelu(x):
        sq = x * x
        th = jnp.tanh(GELU_K * x * (1.0 + GELU_C * sq))
        low = 0.5 * (1.0 + th)
        return x * low, low, th, sq

    for r in range(N_LOSS):
        ok = valid(r - 2)
        both = dot(band_ref[r * CH : (r + 1) * CH, :], taps_a, 1, 0)
        other = dot(band_ref[r * CH + half : (r + 1) * CH, :], taps_b, 1, 0)
        for side in range(2):
            cols = slice(side * CH, (side + 1) * CH)
            g, a, t = both[:half, cols], both[half:, cols], other[:, cols]
            d_disc = (heads_ref[:half, :] * ok) * (0.2 + 0.8 * sigmoid(g))
            fa, low, th, sq = gelu(a)
            fb = gelu(t)[0]
            inv_a = lax.rsqrt(jnp.sum(fa * fa, axis=0, keepdims=True) * (1.0 / half) + NORM_EPS)
            inv_b = lax.rsqrt(jnp.sum(fb * fb, axis=0, keepdims=True) * (1.0 / half) + NORM_EPS)
            na = fa * inv_a
            up = (heads_ref[half:, :] * ok) * (na - fb * inv_b)
            mean = jnp.sum(up * na, axis=0, keepdims=True) * (1.0 / half)
            d_feat = inv_a * (up - na * mean)
            rise = low + 0.5 * a * (1.0 - th * th) * (GELU_K * (1.0 + 3.0 * GELU_C * sq))
            dall[r * CH : r * CH + half, cols] = d_disc.astype(bf16)
            dall[r * CH + half : (r + 1) * CH, cols] = (d_feat * rise).astype(bf16)

    back = dot(band_t_ref[...], dall[...], 1, 0)
    n = N_GRAD * 8
    diff = (image - true_image)[16 : 16 + n]
    grad_image = (
        shifted(back[:n], -1) + back[n : 2 * n] + shifted(back[2 * n :], 1)
        + diff * lax.rsqrt(diff * diff + CHARB_EPS)
    )
    out_w2 = jnp.concatenate([out_w, out_w], axis=0).astype(bf16)
    grad_out = jnp.zeros((16, CH), f32)
    for q in range(N_GRAD):
        g = grad_image[q * 8 : (q + 1) * 8] * valid(q - 1)
        high = g.astype(bf16).astype(f32)
        pair = jnp.concatenate([high, g - high], axis=0)
        grad_pre = dot(pair.T.astype(bf16), out_w2, 1, 0) * slope[q]
        grad_pre_ref[q] = grad_pre.astype(bf16)
        if 1 <= q <= ROWS_LOC:
            y0[pl.ds((q - 1) * PITCH + 8, COLS), :] = grad_pre
            grad_out = grad_out + dot(pair.astype(bf16), hidden[q - 1], 1, 0)
    grad_out = grad_out[:8] + grad_out[8:]

    lhs, rhs = [], []
    for y in range(ROWS_LOC):
        at = y * PITCH + 8
        lhs.append(
            jnp.concatenate([y0[pl.ds(at + 1 - b, COLS), :] for b in range(3)], axis=1).astype(bf16)
        )
        rhs.append(jnp.concatenate([feats(3 + y + a) for a in range(3)], axis=1))
    lhs, rhs = jnp.concatenate(lhs, axis=0), jnp.concatenate(rhs, axis=0)
    packed[...] = jnp.zeros_like(packed)
    for b in range(3):
        grad = dot(lhs[:, b * CH : (b + 1) * CH], rhs, 0, 0)
        for a in range(3):
            tap = a * 3 + b
            for d in range(8):
                block = grad[d * 16 : (d + 1) * 16, a * CH : (a + 1) * CH]
                start = tap * 16
                while start < tap * 16 + 16:
                    part, inner = divmod(start, 18)
                    count = min(18 - inner, tap * 16 + 16 - start)
                    at = ((d // 2) * 8 + part) * 2 * BLOCK + (d % 2) * BLOCK + inner
                    packed[pl.ds(at, count), :] = block[start - tap * 16 : start - tap * 16 + count]
                    start += count
    for d in range(8):
        for c in range(3):
            line = grad_out[c : c + 1]
            if d:
                line = pltpu.roll(line, CH - 16 * d, 1)
            packed[pl.ds(((d // 2) * 8 + c) * 2 * BLOCK + (d % 2) * BLOCK + 18, 1), :] = line
    piece_ref[...] = packed[...].astype(bf16)


def back_kernel(grad_ref, conv_ref, out_ref, z0, z1, z2):
    bf16, f32 = jnp.bfloat16, jnp.float32
    for buf in (z0, z2):
        for y in range(ROWS_LOC + 1):
            buf[pl.ds(y * PITCH, 8), :] = jnp.zeros((8, CH), f32)
    weights = jnp.concatenate(
        [jnp.concatenate([conv_ref[a, b] for a in range(3)], axis=1) for b in range(3)], axis=0
    )
    for y in range(ROWS_LOC):
        lhs = jnp.concatenate([grad_ref[y + 2 - a] for a in range(3)], axis=1)
        prod = dot(lhs, weights, 1, 1)
        for b, buf in enumerate((z0, z1, z2)):
            buf[pl.ds(y * PITCH + 8, COLS), :] = prod[:, b * CH : (b + 1) * CH]
    for y in range(ROWS_LOC):
        at = y * PITCH + 8
        total = z0[pl.ds(at + 1, COLS), :] + z1[pl.ds(at, COLS), :] + z2[pl.ds(at - 1, COLS), :]
        out_ref[y] = total.astype(bf16)


def first_sum_kernel(in_ref, out_ref):
    total = in_ref[0].astype(jnp.float32)
    for k in range(1, in_ref.shape[0]):
        total = total + in_ref[k].astype(jnp.float32)
    pad = jnp.zeros((PADDED - BLOCK, CH), jnp.float32)
    for half in range(2):
        part = jnp.concatenate([total[half * BLOCK : (half + 1) * BLOCK], pad], axis=0)
        for k in range(8):
            out_ref[half * 8 + k] = part.astype(jnp.bfloat16)


def second_sum_kernel(in_ref, out_ref):
    total = in_ref[0].astype(jnp.float32)
    for k in range(1, in_ref.shape[0]):
        total = total + in_ref[k].astype(jnp.float32)
    for k in range(8):
        out_ref[k] = total


def last_kernel(in_ref, conv_ref, out_ref):
    for k in range(8):
        conv_ref[pl.ds(k * 18, 18), :] = in_ref[k, 0:18, :]
    for c in range(3):
        out_ref[c : c + 1, :] = in_ref[c, 18:19, :16]


def call(kernel, out_shape, scratch=(), smem=0, whole=0, n_in=1, flops=0, name=None, vmem=4):
    specs = [pl.BlockSpec(memory_space=pltpu.SMEM)] * smem
    specs += [pl.BlockSpec(memory_space=pltpu.HBM)] * whole
    specs += [pl.BlockSpec(memory_space=VMEM)] * (n_in - smem - whole)
    many = isinstance(out_shape, tuple)
    return pl.pallas_call(
        kernel,
        out_shape=out_shape,
        in_specs=specs,
        out_specs=tuple(pl.BlockSpec(memory_space=VMEM) for _ in out_shape)
        if many
        else pl.BlockSpec(memory_space=VMEM),
        scratch_shapes=list(scratch),
        cost_estimate=pl.CostEstimate(flops=flops, bytes_accessed=1 << 20, transcendentals=0),
        compiler_params=pltpu.CompilerParams(vmem_limit_bytes=vmem << 20),
        name=name,
    )


def shape(*dims, dtype=jnp.float32):
    return jax.ShapeDtypeStruct(dims, dtype)


def pack(features, targets):
    return call(
        pack_kernel,
        shape(TILE + 64, CH, dtype=jnp.bfloat16),
        scratch=[VMEM((3, ROWS_LOC, COLS), jnp.float32), pltpu.SemaphoreType.DMA((2,))],
        n_in=2,
        whole=2,
        name="pack",
    )(
        pltpu.with_memory_space_constraint(features.reshape(TILE, CH), pltpu.HBM),
        pltpu.with_memory_space_constraint(targets, pltpu.HBM),
    )


def prepare(disc_weight, disc_head, lpips_weight, lpips_lin, out_weight):
    bf16 = jnp.bfloat16
    ahead, back = band_selectors()
    return call(
        prep_kernel,
        (
            shape(N_LOSS * CH, K_BAND, dtype=bf16),
            shape(3 * N_GRAD * 8, N_LOSS * CH, dtype=bf16),
            shape(CH, CH),
            shape(8, CH),
        ),
        scratch=[VMEM((32, CH), jnp.float32)],
        n_in=7,
        flops=1 << 28,
        name="bands",
    )(
        disc_weight, lpips_weight, disc_head.reshape(1, -1), lpips_lin.reshape(1, -1),
        out_weight.T, jnp.asarray(ahead, bf16), jnp.asarray(back, bf16),
    )


def tile_step(tile, near, own, far, conv_weight, band, band_t, heads, out_w):
    f32, bf16 = jnp.float32, jnp.bfloat16
    rows = N_PRE * PITCH + 8
    return call(
        main_kernel,
        (
            shape(3, ROWS_LOC, COLS),
            shape(N_GRAD, COLS, CH, dtype=bf16),
            shape(32 * 2 * BLOCK, CH, dtype=bf16),
        ),
        scratch=[
            VMEM((rows, CH), f32),
            VMEM((rows, CH), f32),
            VMEM((rows, CH), f32),
            VMEM((N_GRAD, COLS, CH), f32),
            VMEM((ROWS_LOC, COLS, CH), bf16),
            VMEM((N_PRE * 8, COLS), f32),
            VMEM((N_LOSS * CH, COLS), bf16),
            VMEM((32 * 2 * BLOCK, CH), f32),
            VMEM((TILE + 64, CH), bf16),
            VMEM((TILE + 64, CH), bf16),
        ],
        smem=1,
        n_in=9,
        flops=1 << 31,
        name="tile",
        vmem=20,
    )(tile, near, own, far, conv_weight, out_w, band, band_t, heads)


def back_step(grad_pre, conv_weight):
    rows = ROWS_LOC * PITCH + 8
    return call(
        back_kernel,
        shape(ROWS_LOC, COLS, CH, dtype=jnp.bfloat16),
        scratch=[VMEM((rows, CH), jnp.float32)] * 3,
        n_in=2,
        flops=1 << 30,
        name="features_back",
        vmem=8,
    )(grad_pre, conv_weight)


def swap(array, axes):
    return lax.all_to_all(array, axes, split_axis=0, concat_axis=0, tiled=True)


def swaps(firsts):
    return [pair for i in firsts for pair in ((i, i + 1), (i + 1, i))]


ROWS = ("zl", "x", "core")


def body(
    features, conv_weight, out_weight, targets, disc_weight, disc_head, lpips_weight, lpips_lin
):
    own = pack(features[0], jnp.transpose(targets[0], (2, 0, 1)))
    near = lax.ppermute(own, ROWS, swaps(range(0, TILES, 2)))
    far = lax.ppermute(own, ROWS, swaps(range(1, TILES - 1, 2)))
    tables = prepare(disc_weight, disc_head, lpips_weight, lpips_lin, out_weight)
    tile = lax.axis_index(ROWS).astype(jnp.int32).reshape(1)
    recon, grad_pre, pieces = tile_step(tile, near, own, far, conv_weight, *tables)
    grad_features = back_step(grad_pre, conv_weight)
    pieces = swap(pieces.reshape(32, 2 * BLOCK, CH), ("y", "x", "core"))
    pieces = call(first_sum_kernel, shape(16, PADDED, CH, dtype=jnp.bfloat16), name="sum_1")(pieces)
    pieces = swap(pieces, ("zh", "zl"))
    pieces = call(second_sum_kernel, shape(8, PADDED, CH), name="sum_2")(pieces)
    pieces = swap(pieces, ("x", "core"))
    grad_conv, grad_out = call(last_kernel, (shape(144, CH), shape(3, 16)), name="join")(pieces)
    return (
        jnp.transpose(recon, (1, 2, 0))[None],
        grad_features[None],
        jnp.transpose(grad_conv.reshape(3, 3, 16, CH), (0, 1, 3, 2)),
        grad_out.T,
    )


def solution(mesh):
    fine = Mesh(mesh.devices.reshape(4, 2, 8, 4, 2), ("y", "zh", "zl", "x", "core"))
    dp = ("y", "zh")
    in_specs = (
        P(dp, ROWS, None, None), P(), P(), P(dp, ROWS, None, None), P(), P(), P(), P(),
    )
    out_specs = (
        P(dp, ROWS, None, None), P(dp, ROWS, None, None), P(None, None, None, dp), P(dp, None),
    )
    return jax.shard_map(body, mesh=fine, in_specs=in_specs, out_specs=out_specs, check_vma=False)
```

```python
import functools

import jax
import jax.numpy as jnp
import numpy as np
from jax import lax
from jax.experimental import pallas as pl
from jax.experimental.pallas import tpu as pltpu
from jax.sharding import Mesh, PartitionSpec as P

ADV_SCALE = 0.5
CHARB_EPS = 0.01
NORM_EPS = 1e-06
GELU_K = 0.7978845608028654
GELU_C = 0.044715

ROWS_LOC = 4
COLS = 256
TILE = ROWS_LOC * COLS
CH = 128
TILES = 64
HEIGHT = ROWS_LOC * TILES
N_PRE = 10
N_LOSS = 8
N_GRAD = 6
PITCH = COLS + 8
K_BAND = 256
BLOCK = 20
PADDED = 24
VMEM = pltpu.VMEM


def band_selectors():
    ahead = np.zeros((32, N_LOSS * K_BAND), np.float32)
    back = np.zeros((N_LOSS * 3 * N_GRAD * 8, 32), np.float32)
    for a in range(3):
        for b in range(3):
            for c in range(3):
                tap = (a * 3 + b) * 3 + c
                for r in range(N_LOSS):
                    ahead[tap, r * K_BAND + b * N_PRE * 8 + (r + a) * 8 + c] = 1.0
                    q = r + a - 2
                    if 0 <= q < N_GRAD:
                        back[r * 3 * N_GRAD * 8 + b * N_GRAD * 8 + q * 8 + c, tap] = 1.0
    return ahead, back


def dot(a, b, ca, cb):
    return lax.dot_general(a, b, (((ca,), (cb,)), ((), ())), preferred_element_type=jnp.float32)


def sigmoid(x):
    return 0.5 * jnp.tanh(0.5 * x) + 0.5


def shifted(x, by):
    lane = lax.broadcasted_iota(jnp.int32, x.shape, 1)
    if by == 1:
        return jnp.where(lane == 0, 0.0, pltpu.roll(x, 1, 1))
    return jnp.where(lane == COLS - 1, 0.0, pltpu.roll(x, COLS - 1, 1))


def pack_kernel(own_ref, truth_ref, out_ref, truth_vmem, sems):
    copy = pltpu.make_async_copy(own_ref, out_ref.at[pl.ds(0, TILE)], sems.at[0])
    copy.start()
    fetch = pltpu.make_async_copy(truth_ref, truth_vmem, sems.at[1])
    fetch.start()
    fetch.wait()
    rows = [
        truth_vmem[c, :, h * CH : (h + 1) * CH] for c in range(3) for h in range(COLS // CH)
    ] + [jnp.zeros((8, CH), jnp.float32)]
    exact = jnp.concatenate(rows, axis=0)
    high = exact.astype(jnp.bfloat16)
    out_ref[pl.ds(TILE, 32), :] = high
    out_ref[pl.ds(TILE + 32, 32), :] = (exact - high.astype(jnp.float32)).astype(jnp.bfloat16)
    copy.wait()


def prep_kernel(
    disc_ref, lpips_ref, head_ref, lin_ref, out_w_ref, ahead_ref, back_ref,
    band_ref, band_t_ref, heads_ref, wide_ref, w27_ref,
):
    w27_ref[...] = jnp.zeros_like(w27_ref)
    for a in range(3):
        for b in range(3):
            pair = jnp.concatenate([disc_ref[a, b], lpips_ref[a, b]], axis=1)
            w27_ref[pl.ds((a * 3 + b) * 3, 3), :] = pair
    w27 = w27_ref[...].astype(jnp.bfloat16)
    size = 3 * N_GRAD * 8
    for r in range(N_LOSS):
        band = dot(w27, ahead_ref[:, r * K_BAND : (r + 1) * K_BAND], 0, 0)
        band_ref[r * CH : (r + 1) * CH, :] = band.astype(jnp.bfloat16)
        back = dot(back_ref[r * size : (r + 1) * size, :], w27, 1, 0)
        band_t_ref[:, r * CH : (r + 1) * CH] = back.astype(jnp.bfloat16)
    line = jnp.concatenate([-ADV_SCALE * head_ref[...], 2.0 * lin_ref[...]], axis=1)
    heads_ref[...] = jnp.broadcast_to(line, (CH, CH)).T
    wide_ref[...] = jnp.zeros_like(wide_ref)
    wide_ref[0:3, :] = out_w_ref[...].astype(jnp.float32)


def main_kernel(
    tile_ref, near_ref, own_ref, far_ref, conv_ref, out_w_ref,
    band_ref, band_t_ref, heads_ref,
    recon_ref, grad_pre_ref, piece_ref,
    y0, y1, y2, slope, hidden, truth, dall, packed, up_ref, down_ref,
):
    bf16, f32 = jnp.bfloat16, jnp.float32

    @pl.when(lax.rem(tile_ref[0], 2) == 0)
    def _():
        up_ref[...] = far_ref[...]
        down_ref[...] = near_ref[...]

    @pl.when(lax.rem(tile_ref[0], 2) == 1)
    def _():
        up_ref[...] = near_ref[...]
        down_ref[...] = far_ref[...]

    first_row = tile_ref[0] * ROWS_LOC

    def valid(row):
        inside = jnp.logical_and(first_row + row >= 0, first_row + row < HEIGHT)
        return jnp.where(inside, 1.0, 0.0).astype(f32)

    def feats(j):
        return (up_ref, own_ref, down_ref)[j // ROWS_LOC][pl.ds(j % ROWS_LOC * COLS, COLS), :]

    for buf in (y0, y2):
        for j in range(N_PRE + 1):
            buf[pl.ds(j * PITCH, 8), :] = jnp.zeros((8, CH), f32)
    weights = jnp.concatenate(
        [jnp.concatenate([conv_ref[a, b] for a in range(3)], axis=0) for b in range(3)], axis=1
    )
    out_w = out_w_ref[...]
    out_w16 = out_w.astype(bf16)
    image = []
    for j in range(N_PRE):
        lhs = jnp.concatenate([feats(j), feats(j + 1), feats(j + 2)], axis=1)
        prod = dot(lhs, weights, 1, 0)
        for b, buf in enumerate((y0, y1, y2)):
            buf[pl.ds(j * PITCH + 8, COLS), :] = prod[:, b * CH : (b + 1) * CH]
    for j in range(N_PRE):
        at = j * PITCH + 8
        pre = y0[pl.ds(at - 1, COLS), :] + y1[pl.ds(at, COLS), :] + y2[pl.ds(at + 1, COLS), :]
        sig = sigmoid(pre)
        act = (pre * sig).astype(bf16)
        if 2 <= j < 2 + N_GRAD:
            slope[j - 2] = sig * (1.0 + pre * (1.0 - sig))
        if 3 <= j < 3 + ROWS_LOC:
            hidden[j - 3] = act
        image.append(dot(out_w16, act, 1, 1) * valid(j - 3))
    for j in range(ROWS_LOC):
        for c in range(3):
            recon_ref[c, j : j + 1, :] = image[j + 3][c : c + 1, :]
    image = jnp.concatenate(image, axis=0)

    truth[...] = jnp.zeros_like(truth)
    targets = [
        ref[pl.ds(TILE, 32), :].astype(f32) + ref[pl.ds(TILE + 32, 32), :].astype(f32)
        for ref in (up_ref, own_ref, down_ref)
    ]
    for j in range(N_PRE):
        src, row = targets[(j + 1) // ROWS_LOC], (j + 1) % ROWS_LOC
        for c in range(3):
            for h in range(COLS // CH):
                at = (c * 2 + h) * ROWS_LOC + row
                truth[j * 8 + c : j * 8 + c + 1, h * CH : (h + 1) * CH] = src[at : at + 1]
    true_image = truth[...]

    def taps(x):
        pad = jnp.zeros((K_BAND - 3 * N_PRE * 8, COLS), f32)
        return jnp.concatenate([shifted(x, 1), x, shifted(x, -1), pad], axis=0).astype(bf16)

    taps_a, taps_b = taps(image), taps(true_image)
    half = CH // 2

    def gelu(x):
        sq = x * x
        th = jnp.tanh(GELU_K * x * (1.0 + GELU_C * sq))
        low = 0.5 * (1.0 + th)
        return x * low, low, th, sq

    for r in range(N_LOSS):
        ok = valid(r - 2)
        both = dot(band_ref[r * CH : (r + 1) * CH, :], taps_a, 1, 0)
        other = dot(band_ref[r * CH + half : (r + 1) * CH, :], taps_b, 1, 0)
        for side in range(2):
            cols = slice(side * CH, (side + 1) * CH)
            g, a, t = both[:half, cols], both[half:, cols], other[:, cols]
            d_disc = (heads_ref[:half, :] * ok) * (0.2 + 0.8 * sigmoid(g))
            fa, low, th, sq = gelu(a)
            fb = gelu(t)[0]
            inv_a = lax.rsqrt(jnp.sum(fa * fa, axis=0, keepdims=True) * (1.0 / half) + NORM_EPS)
            inv_b = lax.rsqrt(jnp.sum(fb * fb, axis=0, keepdims=True) * (1.0 / half) + NORM_EPS)
            na = fa * inv_a
            up = (heads_ref[half:, :] * ok) * (na - fb * inv_b)
            mean = jnp.sum(up * na, axis=0, keepdims=True) * (1.0 / half)
            d_feat = inv_a * (up - na * mean)
            rise = low + 0.5 * a * (1.0 - th * th) * (GELU_K * (1.0 + 3.0 * GELU_C * sq))
            dall[r * CH : r * CH + half, cols] = d_disc.astype(bf16)
            dall[r * CH + half : (r + 1) * CH, cols] = (d_feat * rise).astype(bf16)

    back = dot(band_t_ref[...], dall[...], 1, 0)
    n = N_GRAD * 8
    diff = (image - true_image)[16 : 16 + n]
    grad_image = (
        shifted(back[:n], -1) + back[n : 2 * n] + shifted(back[2 * n :], 1)
        + diff * lax.rsqrt(diff * diff + CHARB_EPS)
    )
    out_w2 = jnp.concatenate([out_w, out_w], axis=0).astype(bf16)
    grad_out = jnp.zeros((16, CH), f32)
    for q in range(N_GRAD):
        g = grad_image[q * 8 : (q + 1) * 8] * valid(q - 1)
        high = g.astype(bf16).astype(f32)
        pair = jnp.concatenate([high, g - high], axis=0)
        grad_pre = dot(pair.T.astype(bf16), out_w2, 1, 0) * slope[q]
        grad_pre_ref[q] = grad_pre.astype(bf16)
        if 1 <= q <= ROWS_LOC:
            y0[pl.ds((q - 1) * PITCH + 8, COLS), :] = grad_pre
            grad_out = grad_out + dot(pair.astype(bf16), hidden[q - 1], 1, 0)
    grad_out = grad_out[:8] + grad_out[8:]

    lhs, rhs = [], []
    for y in range(ROWS_LOC):
        at = y * PITCH + 8
        lhs.append(
            jnp.concatenate([y0[pl.ds(at + 1 - b, COLS), :] for b in range(3)], axis=1).astype(bf16)
        )
        rhs.append(jnp.concatenate([feats(3 + y + a) for a in range(3)], axis=1))
    lhs, rhs = jnp.concatenate(lhs, axis=0), jnp.concatenate(rhs, axis=0)
    packed[...] = jnp.zeros_like(packed)
    for b in range(3):
        grad = dot(lhs[:, b * CH : (b + 1) * CH], rhs, 0, 0)
        for a in range(3):
            tap = a * 3 + b
            for d in range(8):
                block = grad[d * 16 : (d + 1) * 16, a * CH : (a + 1) * CH]
                start = tap * 16
                while start < tap * 16 + 16:
                    part, inner = divmod(start, 18)
                    count = min(18 - inner, tap * 16 + 16 - start)
                    at = ((d // 2) * 8 + part) * 2 * BLOCK + (d % 2) * BLOCK + inner
                    packed[pl.ds(at, count), :] = block[start - tap * 16 : start - tap * 16 + count]
                    start += count
    for d in range(8):
        for c in range(3):
            line = grad_out[c : c + 1]
            if d:
                line = pltpu.roll(line, CH - 16 * d, 1)
            packed[pl.ds(((d // 2) * 8 + c) * 2 * BLOCK + (d % 2) * BLOCK + 18, 1), :] = line
    piece_ref[...] = packed[...].astype(bf16)


def back_kernel(start, grad_ref, conv_ref, out_ref, z0, z1, z2):
    bf16, f32 = jnp.bfloat16, jnp.float32
    for buf in (z0, z2):
        for y in range(out_ref.shape[0] + 1):
            buf[pl.ds(y * PITCH, 8), :] = jnp.zeros((8, CH), f32)
    weights = jnp.concatenate(
        [jnp.concatenate([conv_ref[a, b] for a in range(3)], axis=1) for b in range(3)], axis=0
    )
    for y in range(out_ref.shape[0]):
        lhs = jnp.concatenate([grad_ref[start + y + 2 - a] for a in range(3)], axis=1)
        prod = dot(lhs, weights, 1, 1)
        for b, buf in enumerate((z0, z1, z2)):
            buf[pl.ds(y * PITCH + 8, COLS), :] = prod[:, b * CH : (b + 1) * CH]
    for y in range(out_ref.shape[0]):
        at = y * PITCH + 8
        total = z0[pl.ds(at + 1, COLS), :] + z1[pl.ds(at, COLS), :] + z2[pl.ds(at - 1, COLS), :]
        out_ref[y] = total.astype(bf16)


def first_sum_kernel(in_ref, out_ref):
    total = in_ref[0].astype(jnp.float32)
    for k in range(1, in_ref.shape[0]):
        total = total + in_ref[k].astype(jnp.float32)
    pad = jnp.zeros((PADDED - BLOCK, CH), jnp.float32)
    for half in range(2):
        part = jnp.concatenate([total[half * BLOCK : (half + 1) * BLOCK], pad], axis=0)
        for k in range(8):
            out_ref[half * 8 + k] = part.astype(jnp.bfloat16)


def second_sum_kernel(in_ref, out_ref):
    total = in_ref[0].astype(jnp.float32)
    for k in range(1, in_ref.shape[0]):
        total = total + in_ref[k].astype(jnp.float32)
    for k in range(8):
        out_ref[k] = total


def last_kernel(in_ref, conv_ref, out_ref):
    for k in range(8):
        conv_ref[pl.ds(k * 18, 18), :] = in_ref[k, 0:18, :]
    for c in range(3):
        out_ref[c : c + 1, :] = in_ref[c, 18:19, :16]


def call(kernel, out_shape, scratch=(), smem=0, whole=0, n_in=1, flops=0, name=None, vmem=4):
    specs = [pl.BlockSpec(memory_space=pltpu.SMEM)] * smem
    specs += [pl.BlockSpec(memory_space=pltpu.HBM)] * whole
    specs += [pl.BlockSpec(memory_space=VMEM)] * (n_in - smem - whole)
    many = isinstance(out_shape, tuple)
    return pl.pallas_call(
        kernel,
        out_shape=out_shape,
        in_specs=specs,
        out_specs=tuple(pl.BlockSpec(memory_space=VMEM) for _ in out_shape)
        if many
        else pl.BlockSpec(memory_space=VMEM),
        scratch_shapes=list(scratch),
        cost_estimate=pl.CostEstimate(flops=flops, bytes_accessed=1 << 20, transcendentals=0),
        compiler_params=pltpu.CompilerParams(vmem_limit_bytes=vmem << 20),
        name=name,
    )


def shape(*dims, dtype=jnp.float32):
    return jax.ShapeDtypeStruct(dims, dtype)


def pack(features, targets):
    return call(
        pack_kernel,
        shape(TILE + 64, CH, dtype=jnp.bfloat16),
        scratch=[VMEM((3, ROWS_LOC, COLS), jnp.float32), pltpu.SemaphoreType.DMA((2,))],
        n_in=2,
        whole=2,
        name="pack",
    )(
        pltpu.with_memory_space_constraint(features.reshape(TILE, CH), pltpu.HBM),
        pltpu.with_memory_space_constraint(targets, pltpu.HBM),
    )


def prepare(disc_weight, disc_head, lpips_weight, lpips_lin, out_weight):
    bf16 = jnp.bfloat16
    ahead, back = band_selectors()
    return call(
        prep_kernel,
        (
            shape(N_LOSS * CH, K_BAND, dtype=bf16),
            shape(3 * N_GRAD * 8, N_LOSS * CH, dtype=bf16),
            shape(CH, CH),
            shape(8, CH),
        ),
        scratch=[VMEM((32, CH), jnp.float32)],
        n_in=7,
        flops=1 << 28,
        name="bands",
    )(
        disc_weight, lpips_weight, disc_head.reshape(1, -1), lpips_lin.reshape(1, -1),
        out_weight.T, jnp.asarray(ahead, bf16), jnp.asarray(back, bf16),
    )


def tile_step(tile, near, own, far, conv_weight, band, band_t, heads, out_w):
    f32, bf16 = jnp.float32, jnp.bfloat16
    rows = N_PRE * PITCH + 8
    return call(
        main_kernel,
        (
            shape(3, ROWS_LOC, COLS),
            shape(N_GRAD, COLS, CH, dtype=bf16),
            shape(32 * 2 * BLOCK, CH, dtype=bf16),
        ),
        scratch=[
            VMEM((rows, CH), f32),
            VMEM((rows, CH), f32),
            VMEM((rows, CH), f32),
            VMEM((N_GRAD, COLS, CH), f32),
            VMEM((ROWS_LOC, COLS, CH), bf16),
            VMEM((N_PRE * 8, COLS), f32),
            VMEM((N_LOSS * CH, COLS), bf16),
            VMEM((32 * 2 * BLOCK, CH), f32),
            VMEM((TILE + 64, CH), bf16),
            VMEM((TILE + 64, CH), bf16),
        ],
        smem=1,
        n_in=9,
        flops=1 << 31,
        name="tile",
        vmem=20,
    )(tile, near, own, far, conv_weight, out_w, band, band_t, heads)


def back_step(start, count, grad_pre, conv_weight):
    rows = count * PITCH + 8
    return call(
        functools.partial(back_kernel, start),
        shape(count, COLS, CH, dtype=jnp.bfloat16),
        scratch=[VMEM((rows, CH), jnp.float32)] * 3,
        n_in=2,
        flops=1 << 30,
        name="features_back",
        vmem=8,
    )(grad_pre, conv_weight)


def swap(array, axes):
    return lax.all_to_all(array, axes, split_axis=0, concat_axis=0, tiled=True)


def swaps(firsts):
    return [pair for i in firsts for pair in ((i, i + 1), (i + 1, i))]


ROWS = ("zl", "x", "core")


def body(
    features, conv_weight, out_weight, targets, disc_weight, disc_head, lpips_weight, lpips_lin
):
    own = pack(features[0], jnp.transpose(targets[0], (2, 0, 1)))
    near = lax.ppermute(own, ROWS, swaps(range(0, TILES, 2)))
    far = lax.ppermute(own, ROWS, swaps(range(1, TILES - 1, 2)))
    tables = prepare(disc_weight, disc_head, lpips_weight, lpips_lin, out_weight)
    tile = lax.axis_index(ROWS).astype(jnp.int32).reshape(1)
    recon, grad_pre, pieces = tile_step(tile, near, own, far, conv_weight, *tables)
    grad_1 = back_step(0, 1, grad_pre, conv_weight)
    pieces = swap(pieces.reshape(32, 2 * BLOCK, CH), ("y", "x", "core"))
    pieces, grad_1 = lax.optimization_barrier((pieces, grad_1))
    pieces = call(first_sum_kernel, shape(16, PADDED, CH, dtype=jnp.bfloat16), name="sum_1")(pieces)
    pieces, grad_pre = lax.optimization_barrier((pieces, grad_pre))
    grad_2 = back_step(1, 1, grad_pre, conv_weight)
    pieces = swap(pieces, ("zh", "zl"))
    pieces, grad_2 = lax.optimization_barrier((pieces, grad_2))
    pieces = call(second_sum_kernel, shape(8, PADDED, CH), name="sum_2")(pieces)
    pieces, grad_pre = lax.optimization_barrier((pieces, grad_pre))
    grad_3 = back_step(2, 2, grad_pre, conv_weight)
    pieces = swap(pieces, ("x", "core"))
    grad_features = jnp.concatenate([grad_1, grad_2, grad_3], axis=0)
    grad_conv, grad_out = call(last_kernel, (shape(144, CH), shape(3, 16)), name="join")(pieces)
    return (
        jnp.transpose(recon, (1, 2, 0))[None],
        grad_features[None],
        jnp.transpose(grad_conv.reshape(3, 3, 16, CH), (0, 1, 3, 2)),
        grad_out.T,
    )


def solution(mesh):
    fine = Mesh(mesh.devices.reshape(4, 2, 8, 4, 2), ("y", "zh", "zl", "x", "core"))
    dp = ("y", "zh")
    in_specs = (
        P(dp, ROWS, None, None), P(), P(), P(dp, ROWS, None, None), P(), P(), P(), P(),
    )
    out_specs = (
        P(dp, ROWS, None, None), P(dp, ROWS, None, None), P(None, None, None, dp), P(dp, None),
    )
    return jax.shard_map(body, mesh=fine, in_specs=in_specs, out_specs=out_specs, check_vma=False)
```

```python
import functools

import jax
import jax.numpy as jnp
import numpy as np
from jax import lax
from jax.experimental import pallas as pl
from jax.experimental.pallas import tpu as pltpu
from jax.sharding import Mesh, PartitionSpec as P

ADV_SCALE = 0.5
CHARB_EPS = 0.01
NORM_EPS = 1e-06
GELU_K = 0.7978845608028654
GELU_C = 0.044715

ROWS_LOC = 4
COLS = 256
TILE = ROWS_LOC * COLS
CH = 128
TILES = 64
HEIGHT = ROWS_LOC * TILES
N_PRE = 10
N_LOSS = 8
N_GRAD = 6
PITCH = COLS + 8
K_BAND = 256
BLOCK = 20
PADDED = 24
VMEM = pltpu.VMEM


def band_selectors():
    ahead = np.zeros((32, N_LOSS * K_BAND), np.float32)
    back = np.zeros((N_LOSS * 3 * N_GRAD * 8, 32), np.float32)
    for a in range(3):
        for b in range(3):
            for c in range(3):
                tap = (a * 3 + b) * 3 + c
                for r in range(N_LOSS):
                    ahead[tap, r * K_BAND + b * N_PRE * 8 + (r + a) * 8 + c] = 1.0
                    q = r + a - 2
                    if 0 <= q < N_GRAD:
                        back[r * 3 * N_GRAD * 8 + b * N_GRAD * 8 + q * 8 + c, tap] = 1.0
    return ahead, back


def dot(a, b, ca, cb):
    return lax.dot_general(a, b, (((ca,), (cb,)), ((), ())), preferred_element_type=jnp.float32)


def sigmoid(x):
    return 0.5 * jnp.tanh(0.5 * x) + 0.5


def shifted(x, by):
    lane = lax.broadcasted_iota(jnp.int32, x.shape, 1)
    if by == 1:
        return jnp.where(lane == 0, 0.0, pltpu.roll(x, 1, 1))
    return jnp.where(lane == COLS - 1, 0.0, pltpu.roll(x, COLS - 1, 1))


def pack_kernel(own_ref, truth_ref, out_ref, truth_vmem, sems):
    copy = pltpu.make_async_copy(own_ref, out_ref.at[pl.ds(0, TILE)], sems.at[0])
    copy.start()
    fetch = pltpu.make_async_copy(truth_ref, truth_vmem, sems.at[1])
    fetch.start()
    fetch.wait()
    rows = [
        truth_vmem[c, :, h * CH : (h + 1) * CH] for c in range(3) for h in range(COLS // CH)
    ] + [jnp.zeros((8, CH), jnp.float32)]
    exact = jnp.concatenate(rows, axis=0)
    high = exact.astype(jnp.bfloat16)
    out_ref[pl.ds(TILE, 32), :] = high
    out_ref[pl.ds(TILE + 32, 32), :] = (exact - high.astype(jnp.float32)).astype(jnp.bfloat16)
    copy.wait()


def prep_kernel(
    disc_ref, lpips_ref, head_ref, lin_ref, out_w_ref, ahead_ref, back_ref, conv_ref,
    band_ref, band_t_ref, heads_ref, wide_ref, two_ref, w27_ref,
):
    w27_ref[...] = jnp.zeros_like(w27_ref)
    for a in range(3):
        for b in range(3):
            pair = jnp.concatenate([disc_ref[a, b], lpips_ref[a, b]], axis=1)
            w27_ref[pl.ds((a * 3 + b) * 3, 3), :] = pair
    w27 = w27_ref[...].astype(jnp.bfloat16)
    size = 3 * N_GRAD * 8
    for r in range(N_LOSS):
        band = dot(w27, ahead_ref[:, r * K_BAND : (r + 1) * K_BAND], 0, 0)
        band_ref[r * CH : r * CH + CH // 2, :] = (0.5 * band[: CH // 2]).astype(jnp.bfloat16)
        band_ref[r * CH + CH // 2 : (r + 1) * CH, :] = band[CH // 2 :].astype(jnp.bfloat16)
        back = dot(back_ref[r * size : (r + 1) * size, :], w27, 1, 0)
        band_t_ref[:, r * CH : (r + 1) * CH] = back.astype(jnp.bfloat16)
    line = jnp.concatenate([-0.4 * ADV_SCALE * head_ref[...], 2.0 * lin_ref[...]], axis=1)
    heads_ref[...] = jnp.broadcast_to(line, (CH, CH)).T
    wide_ref[...] = jnp.zeros_like(wide_ref)
    wide_ref[0:3, :] = out_w_ref[...].astype(jnp.float32)
    zero = jnp.zeros((CH, CH), jnp.bfloat16)
    for b in range(3):
        for k in range(4):
            two_ref[b, k * CH : (k + 1) * CH, :CH] = conv_ref[k, b] if k < 3 else zero
            two_ref[b, k * CH : (k + 1) * CH, CH:] = conv_ref[k - 1, b] if k else zero


def main_kernel(
    tile_ref, near_ref, own_ref, far_ref, two_ref, out_w_ref,
    band_ref, band_t_ref, heads_ref,
    recon_ref, grad_pre_ref, piece_ref,
    y0, y1, y2, slope, hidden, truth, dall, packed, up_ref, down_ref,
):
    bf16, f32 = jnp.bfloat16, jnp.float32

    @pl.when(lax.rem(tile_ref[0], 2) == 0)
    def _():
        up_ref[...] = far_ref[...]
        down_ref[...] = near_ref[...]

    @pl.when(lax.rem(tile_ref[0], 2) == 1)
    def _():
        up_ref[...] = near_ref[...]
        down_ref[...] = far_ref[...]

    first_row = tile_ref[0] * ROWS_LOC

    def valid(row):
        inside = jnp.logical_and(first_row + row >= 0, first_row + row < HEIGHT)
        return jnp.where(inside, 1.0, 0.0).astype(f32)

    def feats(j):
        return (up_ref, own_ref, down_ref)[j // ROWS_LOC][pl.ds(j % ROWS_LOC * COLS, COLS), :]

    for buf in (y0, y2):
        for j in range(N_PRE + 1):
            buf[pl.ds(j * PITCH, 8), :] = jnp.zeros((8, CH), f32)
    out_w = out_w_ref[...]
    out_w16 = out_w.astype(bf16)
    image = []
    for j in range(0, N_PRE, 2):
        lhs = jnp.concatenate([feats(j + k) for k in range(4)], axis=1)
        for b, buf in enumerate((y0, y1, y2)):
            prod = dot(lhs, two_ref[b], 1, 0)
            buf[pl.ds(j * PITCH + 8, COLS), :] = prod[:, :CH]
            buf[pl.ds((j + 1) * PITCH + 8, COLS), :] = prod[:, CH:]
    for j in range(N_PRE):
        at = j * PITCH + 8
        pre = y0[pl.ds(at - 1, COLS), :] + y1[pl.ds(at, COLS), :] + y2[pl.ds(at + 1, COLS), :]
        sig = sigmoid(pre)
        act = (pre * sig).astype(bf16)
        if 2 <= j < 2 + N_GRAD:
            slope[j - 2] = sig * (1.0 + pre * (1.0 - sig))
        if 3 <= j < 3 + ROWS_LOC:
            hidden[j - 3] = act
        image.append(dot(out_w16, act, 1, 1) * valid(j - 3))
    for j in range(ROWS_LOC):
        for c in range(3):
            recon_ref[c, j : j + 1, :] = image[j + 3][c : c + 1, :]
    image = jnp.concatenate(image, axis=0)

    truth[...] = jnp.zeros_like(truth)
    targets = [
        ref[pl.ds(TILE, 32), :].astype(f32) + ref[pl.ds(TILE + 32, 32), :].astype(f32)
        for ref in (up_ref, own_ref, down_ref)
    ]
    for j in range(N_PRE):
        src, row = targets[(j + 1) // ROWS_LOC], (j + 1) % ROWS_LOC
        for c in range(3):
            for h in range(COLS // CH):
                at = (c * 2 + h) * ROWS_LOC + row
                truth[j * 8 + c : j * 8 + c + 1, h * CH : (h + 1) * CH] = src[at : at + 1]
    true_image = truth[...]

    def taps(x):
        pad = jnp.zeros((K_BAND - 3 * N_PRE * 8, COLS), f32)
        return jnp.concatenate([shifted(x, 1), x, shifted(x, -1), pad], axis=0).astype(bf16)

    taps_a, taps_b = taps(image), taps(true_image)
    half = CH // 2

    def gelu(x):
        sq = x * x
        th = jnp.tanh(x * (GELU_K + (GELU_K * GELU_C) * sq))
        rise = 1.0 + th
        return x * rise, rise, th, sq

    def norm(twice):
        mean = jnp.sum(twice * twice, axis=0, keepdims=True) * (1.0 / half)
        return lax.rsqrt(mean + 4.0 * NORM_EPS)

    for r in range(N_LOSS):
        inside = 2 <= r < 2 + ROWS_LOC
        ok = 1.0 if inside else valid(r - 2)
        both = dot(band_ref[r * CH : (r + 1) * CH, :], taps_a, 1, 0)
        other = dot(band_ref[r * CH + half : (r + 1) * CH, :], taps_b, 1, 0)
        for side in range(2):
            cols = slice(side * CH, (side + 1) * CH)
            g, a, t = both[:half, cols], both[half:, cols], other[:, cols]
            head = heads_ref[:half, :] if inside else heads_ref[:half, :] * ok
            d_disc = head * (1.5 + jnp.tanh(g))
            fa, rise, th, sq = gelu(a)
            fb = gelu(t)[0]
            inv_a, inv_b = norm(fa), norm(fb)
            na = fa * inv_a
            up = heads_ref[half:, :] * (na - fb * inv_b)
            mean = jnp.sum(up * na, axis=0, keepdims=True) * (1.0 / half)
            d_feat = (inv_a * ok) * (up - na * mean)
            slant = rise + fa * (1.0 - th) * (GELU_K + (3.0 * GELU_K * GELU_C) * sq)
            dall[r * CH : r * CH + half, cols] = d_disc.astype(bf16)
            dall[r * CH + half : (r + 1) * CH, cols] = (d_feat * slant).astype(bf16)

    back = dot(band_t_ref[...], dall[...], 1, 0)
    n = N_GRAD * 8
    diff = (image - true_image)[16 : 16 + n]
    grad_image = (
        shifted(back[:n], -1) + back[n : 2 * n] + shifted(back[2 * n :], 1)
        + diff * lax.rsqrt(diff * diff + CHARB_EPS)
    )
    out_w2 = jnp.concatenate([out_w, out_w], axis=0).astype(bf16)
    grad_out = jnp.zeros((16, CH), f32)
    for q in range(N_GRAD):
        g = grad_image[q * 8 : (q + 1) * 8] * valid(q - 1)
        high = g.astype(bf16).astype(f32)
        pair = jnp.concatenate([high, g - high], axis=0)
        grad_pre = dot(pair.T.astype(bf16), out_w2, 1, 0) * slope[q]
        grad_pre_ref[q] = grad_pre.astype(bf16)
        if 1 <= q <= ROWS_LOC:
            y0[pl.ds((q - 1) * PITCH + 8, COLS), :] = grad_pre
            grad_out = grad_out + dot(pair.astype(bf16), hidden[q - 1], 1, 0)
    grad_out = grad_out[:8] + grad_out[8:]

    lhs, rhs = [], []
    for y in range(ROWS_LOC):
        at = y * PITCH + 8
        lhs.append(
            jnp.concatenate([y0[pl.ds(at + 1 - b, COLS), :] for b in range(3)], axis=1).astype(bf16)
        )
        rhs.append(jnp.concatenate([feats(3 + y + a) for a in range(3)], axis=1))
    lhs, rhs = jnp.concatenate(lhs, axis=0), jnp.concatenate(rhs, axis=0)
    for k in range(64):
        packed[pl.ds(k * BLOCK + 18, 2), :] = jnp.zeros((2, CH), f32)
    for b in range(3):
        grad = dot(lhs[:, b * CH : (b + 1) * CH], rhs, 0, 0)
        for a in range(3):
            tap = a * 3 + b
            for d in range(8):
                block = grad[d * 16 : (d + 1) * 16, a * CH : (a + 1) * CH]
                start = tap * 16
                while start < tap * 16 + 16:
                    part, inner = divmod(start, 18)
                    count = min(18 - inner, tap * 16 + 16 - start)
                    at = ((d // 2) * 8 + part) * 2 * BLOCK + (d % 2) * BLOCK + inner
                    packed[pl.ds(at, count), :] = block[start - tap * 16 : start - tap * 16 + count]
                    start += count
    for d in range(8):
        for c in range(3):
            line = grad_out[c : c + 1]
            if d:
                line = pltpu.roll(line, CH - 16 * d, 1)
            packed[pl.ds(((d // 2) * 8 + c) * 2 * BLOCK + (d % 2) * BLOCK + 18, 1), :] = line
    piece_ref[...] = packed[...].astype(bf16)


def back_kernel(grad_ref, conv_ref, out_ref, z0, z1, z2):
    bf16, f32 = jnp.bfloat16, jnp.float32
    for buf in (z0, z2):
        for y in range(ROWS_LOC + 1):
            buf[pl.ds(y * PITCH, 8), :] = jnp.zeros((8, CH), f32)
    weights = jnp.concatenate(
        [jnp.concatenate([conv_ref[a, b] for a in range(3)], axis=1) for b in range(3)], axis=0
    )
    for y in range(ROWS_LOC):
        lhs = jnp.concatenate([grad_ref[y + 2 - a] for a in range(3)], axis=1)
        prod = dot(lhs, weights, 1, 1)
        for b, buf in enumerate((z0, z1, z2)):
            buf[pl.ds(y * PITCH + 8, COLS), :] = prod[:, b * CH : (b + 1) * CH]
    for y in range(ROWS_LOC):
        at = y * PITCH + 8
        total = z0[pl.ds(at + 1, COLS), :] + z1[pl.ds(at, COLS), :] + z2[pl.ds(at - 1, COLS), :]
        out_ref[y] = total.astype(bf16)


def first_sum_kernel(in_ref, out_ref):
    total = in_ref[0].astype(jnp.float32)
    for k in range(1, in_ref.shape[0]):
        total = total + in_ref[k].astype(jnp.float32)
    pad = jnp.zeros((PADDED - BLOCK, CH), jnp.float32)
    for half in range(2):
        part = jnp.concatenate([total[half * BLOCK : (half + 1) * BLOCK], pad], axis=0)
        for k in range(8):
            out_ref[half * 8 + k] = part.astype(jnp.bfloat16)


def second_sum_kernel(in_ref, out_ref):
    total = in_ref[0].astype(jnp.float32)
    for k in range(1, in_ref.shape[0]):
        total = total + in_ref[k].astype(jnp.float32)
    for k in range(8):
        out_ref[k] = total


def last_kernel(in_ref, conv_ref, out_ref):
    for k in range(8):
        conv_ref[pl.ds(k * 18, 18), :] = in_ref[k, 0:18, :]
    for c in range(3):
        out_ref[c : c + 1, :] = in_ref[c, 18:19, :16]


def call(kernel, out_shape, scratch=(), smem=0, whole=0, n_in=1, flops=0, name=None, vmem=4):
    specs = [pl.BlockSpec(memory_space=pltpu.SMEM)] * smem
    specs += [pl.BlockSpec(memory_space=pltpu.HBM)] * whole
    specs += [pl.BlockSpec(memory_space=VMEM)] * (n_in - smem - whole)
    many = isinstance(out_shape, tuple)
    return pl.pallas_call(
        kernel,
        out_shape=out_shape,
        in_specs=specs,
        out_specs=tuple(pl.BlockSpec(memory_space=VMEM) for _ in out_shape)
        if many
        else pl.BlockSpec(memory_space=VMEM),
        scratch_shapes=list(scratch),
        cost_estimate=pl.CostEstimate(flops=flops, bytes_accessed=1 << 20, transcendentals=0),
        compiler_params=pltpu.CompilerParams(vmem_limit_bytes=vmem << 20),
        name=name,
    )


def shape(*dims, dtype=jnp.float32):
    return jax.ShapeDtypeStruct(dims, dtype)


def pack(features, targets):
    return call(
        pack_kernel,
        shape(TILE + 64, CH, dtype=jnp.bfloat16),
        scratch=[VMEM((3, ROWS_LOC, COLS), jnp.float32), pltpu.SemaphoreType.DMA((2,))],
        n_in=2,
        whole=2,
        name="pack",
    )(
        pltpu.with_memory_space_constraint(features.reshape(TILE, CH), pltpu.HBM),
        pltpu.with_memory_space_constraint(targets, pltpu.HBM),
    )


def prepare(conv_weight, disc_weight, disc_head, lpips_weight, lpips_lin, out_weight):
    bf16 = jnp.bfloat16
    ahead, back = band_selectors()
    return call(
        prep_kernel,
        (
            shape(N_LOSS * CH, K_BAND, dtype=bf16),
            shape(3 * N_GRAD * 8, N_LOSS * CH, dtype=bf16),
            shape(CH, CH),
            shape(8, CH),
            shape(3, 4 * CH, 2 * CH, dtype=bf16),
        ),
        scratch=[VMEM((32, CH), jnp.float32)],
        n_in=8,
        flops=1 << 28,
        name="bands",
    )(
        disc_weight, lpips_weight, disc_head.reshape(1, -1), lpips_lin.reshape(1, -1),
        out_weight.T, jnp.asarray(ahead, bf16), jnp.asarray(back, bf16), conv_weight,
    )


def tile_step(tile, near, own, far, band, band_t, heads, out_w, two):
    f32, bf16 = jnp.float32, jnp.bfloat16
    rows = N_PRE * PITCH + 8
    return call(
        main_kernel,
        (
            shape(3, ROWS_LOC, COLS),
            shape(N_GRAD, COLS, CH, dtype=bf16),
            shape(32 * 2 * BLOCK, CH, dtype=bf16),
        ),
        scratch=[
            VMEM((rows, CH), f32),
            VMEM((rows, CH), f32),
            VMEM((rows, CH), f32),
            VMEM((N_GRAD, COLS, CH), f32),
            VMEM((ROWS_LOC, COLS, CH), bf16),
            VMEM((N_PRE * 8, COLS), f32),
            VMEM((N_LOSS * CH, COLS), bf16),
            VMEM((32 * 2 * BLOCK, CH), f32),
            VMEM((TILE + 64, CH), bf16),
            VMEM((TILE + 64, CH), bf16),
        ],
        smem=1,
        n_in=9,
        flops=1 << 31,
        name="tile",
        vmem=20,
    )(tile, near, own, far, two, out_w, band, band_t, heads)


def back_step(grad_pre, conv_weight):
    rows = ROWS_LOC * PITCH + 8
    return call(
        back_kernel,
        shape(ROWS_LOC, COLS, CH, dtype=jnp.bfloat16),
        scratch=[VMEM((rows, CH), jnp.float32)] * 3,
        n_in=2,
        flops=1 << 30,
        name="features_back",
        vmem=8,
    )(grad_pre, conv_weight)


def swap(array, axes):
    return lax.all_to_all(array, axes, split_axis=0, concat_axis=0, tiled=True)


def swaps(firsts):
    return [pair for i in firsts for pair in ((i, i + 1), (i + 1, i))]


ROWS = ("zl", "x", "core")


def body(
    features, conv_weight, out_weight, targets, disc_weight, disc_head, lpips_weight, lpips_lin
):
    own = pack(features[0], jnp.transpose(targets[0], (2, 0, 1)))
    near = lax.ppermute(own, ROWS, swaps(range(0, TILES, 2)))
    far = lax.ppermute(own, ROWS, swaps(range(1, TILES - 1, 2)))
    tables = prepare(
        conv_weight, disc_weight, disc_head, lpips_weight, lpips_lin, out_weight
    )
    tile = lax.axis_index(ROWS).astype(jnp.int32).reshape(1)
    recon, grad_pre, pieces = tile_step(tile, near, own, far, *tables)
    pieces = swap(pieces.reshape(32, 2 * BLOCK, CH), ("y", "x", "core"))
    pieces = call(first_sum_kernel, shape(16, PADDED, CH, dtype=jnp.bfloat16), name="sum_1")(pieces)
    pieces, grad_pre = lax.optimization_barrier((pieces, grad_pre))
    grad_features = back_step(grad_pre, conv_weight)
    pieces = swap(pieces, ("zh", "zl"))
    pieces, grad_features = lax.optimization_barrier((pieces, grad_features))
    pieces = call(second_sum_kernel, shape(8, PADDED, CH), name="sum_2")(pieces)
    pieces = swap(pieces, ("x", "core"))
    grad_conv, grad_out = call(last_kernel, (shape(144, CH), shape(3, 16)), name="join")(pieces)
    return (
        jnp.transpose(recon, (1, 2, 0))[None],
        grad_features[None],
        jnp.transpose(grad_conv.reshape(3, 3, 16, CH), (0, 1, 3, 2)),
        grad_out.T,
    )


def solution(mesh):
    fine = Mesh(mesh.devices.reshape(4, 2, 8, 4, 2), ("y", "zh", "zl", "x", "core"))
    dp = ("y", "zh")
    in_specs = (
        P(dp, ROWS, None, None), P(), P(), P(dp, ROWS, None, None), P(), P(), P(), P(),
    )
    out_specs = (
        P(dp, ROWS, None, None), P(dp, ROWS, None, None), P(None, None, None, dp), P(dp, None),
    )
    return jax.shard_map(body, mesh=fine, in_specs=in_specs, out_specs=out_specs, check_vma=False)
```

```python
import jax
import jax.numpy as jnp
from jax import lax
from jax.experimental import pallas as pl
from jax.experimental.pallas import tpu as pltpu
from jax.sharding import Mesh, PartitionSpec as P

ADV_SCALE = 0.5
CHARB_EPS = 0.01
NORM_EPS = 1e-06
GELU_K = 0.7978845608028654
GELU_C = 0.044715

ROWS_LOC = 4
COLS = 256
TILE = ROWS_LOC * COLS
CH = 128
TILES = 64
HEIGHT = ROWS_LOC * TILES
HALO = 3
SLAB = HALO * COLS
N_PRE = 8
N_LOSS = 6
N_GRAD = 4
PITCH = COLS + 8
K_BAND = 256
BLOCK = 20
PADDED = 24
VMEM = pltpu.VMEM


def select_ahead(r):
    lane = lax.broadcasted_iota(jnp.int32, (32, K_BAND), 1)
    b, j, c = lane // (N_PRE * 8), (lane // 8) % N_PRE, lane % 8
    return chosen(lax.broadcasted_iota(jnp.int32, (32, K_BAND), 0), j - r, b, c)


def select_back(r):
    dims = (3 * N_GRAD * 8, 32)
    line = lax.broadcasted_iota(jnp.int32, dims, 0)
    b, q, c = line // (N_GRAD * 8), (line // 8) % N_GRAD, line % 8
    return chosen(lax.broadcasted_iota(jnp.int32, dims, 1), q + 2 - r, b, c)


def chosen(tap, a, b, c):
    real = jnp.logical_and(jnp.logical_and(a >= 0, a < 3), jnp.logical_and(b < 3, c < 3))
    hit = jnp.logical_and(real, tap == 9 * a + 3 * b + c)
    return jnp.where(hit, 1.0, 0.0).astype(jnp.bfloat16)


def dot(a, b, ca, cb):
    return lax.dot_general(a, b, (((ca,), (cb,)), ((), ())), preferred_element_type=jnp.float32)


def sigmoid(x):
    return 0.5 * jnp.tanh(0.5 * x) + 0.5


def shifted(x, by):
    lane = lax.broadcasted_iota(jnp.int32, x.shape, 1)
    if by == 1:
        return jnp.where(lane == 0, 0.0, pltpu.roll(x, 1, 1))
    return jnp.where(lane == COLS - 1, 0.0, pltpu.roll(x, COLS - 1, 1))


def pack_kernel(tile_ref, own_ref, truth_ref, near_ref, far_ref, truth_vmem, sems):
    first = lax.rem(tile_ref[0], 2) == 0
    fetch = pltpu.make_async_copy(truth_ref, truth_vmem, sems.at[2])
    fetch.start()

    def slabs(top_ref, bottom_ref):
        top = pltpu.make_async_copy(
            own_ref.at[pl.ds(0, SLAB)], top_ref.at[pl.ds(0, SLAB)], sems.at[0]
        )
        bottom = pltpu.make_async_copy(
            own_ref.at[pl.ds(COLS, SLAB)], bottom_ref.at[pl.ds(0, SLAB)], sems.at[1]
        )
        top.start()
        bottom.start()
        fetch.wait()
        rows = [
            truth_vmem[c, :, h * CH : (h + 1) * CH] for c in range(3) for h in range(COLS // CH)
        ] + [jnp.zeros((8, CH), jnp.float32)]
        high = jnp.concatenate(rows, axis=0).astype(jnp.bfloat16)
        near_ref[pl.ds(SLAB, 32), :] = high
        far_ref[pl.ds(SLAB, 32), :] = high
        top.wait()
        bottom.wait()

    @pl.when(first)
    def _():
        slabs(far_ref, near_ref)

    @pl.when(jnp.logical_not(first))
    def _():
        slabs(near_ref, far_ref)


def prep_kernel(
    disc_ref, lpips_ref, head_ref, lin_ref, out_w_ref, conv_ref,
    band_ref, band_t_ref, heads_ref, wide_ref, two_ref, w27_ref,
):
    w27_ref[...] = jnp.zeros_like(w27_ref)
    for a in range(3):
        for b in range(3):
            pair = jnp.concatenate([disc_ref[a, b], lpips_ref[a, b]], axis=1)
            w27_ref[pl.ds((a * 3 + b) * 3, 3), :] = pair
    w27 = w27_ref[...].astype(jnp.bfloat16)
    for r in range(N_LOSS):
        band = dot(w27, select_ahead(r), 0, 0)
        band_ref[r * CH : r * CH + CH // 2, :] = (0.5 * band[: CH // 2]).astype(jnp.bfloat16)
        band_ref[r * CH + CH // 2 : (r + 1) * CH, :] = band[CH // 2 :].astype(jnp.bfloat16)
        back = dot(select_back(r), w27, 1, 0)
        band_t_ref[:, r * CH : (r + 1) * CH] = back.astype(jnp.bfloat16)
    line = jnp.concatenate([-0.4 * ADV_SCALE * head_ref[...], 2.0 * lin_ref[...]], axis=1)
    heads_ref[...] = jnp.broadcast_to(line, (CH, CH)).T
    wide_ref[...] = jnp.zeros_like(wide_ref)
    wide_ref[0:3, :] = out_w_ref[...].astype(jnp.float32)
    zero = jnp.zeros((CH, CH), jnp.bfloat16)
    for b in range(3):
        for k in range(4):
            two_ref[b, k * CH : (k + 1) * CH, :CH] = conv_ref[k, b] if k < 3 else zero
            two_ref[b, k * CH : (k + 1) * CH, CH:] = conv_ref[k - 1, b] if k else zero


def main_kernel(
    tile_ref, far_ref, own_ref, truth_ref, near_ref, two_ref, out_w_ref,
    band_ref, band_t_ref, heads_ref,
    recon_ref, grad_pre_ref, near_edge_ref, far_edge_ref, piece_ref,
    y0, y1, y2, slope, hidden, truth, dall, packed, up_ref, down_ref,
):
    bf16, f32 = jnp.bfloat16, jnp.float32

    first = lax.rem(tile_ref[0], 2) == 0

    @pl.when(first)
    def _():
        up_ref[...] = far_ref[...]
        down_ref[...] = near_ref[...]

    @pl.when(jnp.logical_not(first))
    def _():
        up_ref[...] = near_ref[...]
        down_ref[...] = far_ref[...]

    first_row = tile_ref[0] * ROWS_LOC

    def valid(row):
        inside = jnp.logical_and(first_row + row >= 0, first_row + row < HEIGHT)
        return jnp.where(inside, 1.0, 0.0).astype(f32)

    def feats(j):
        if j < HALO:
            return up_ref[pl.ds(j * COLS, COLS), :]
        if j < HALO + ROWS_LOC:
            return own_ref[pl.ds((j - HALO) * COLS, COLS), :]
        return down_ref[pl.ds((j - HALO - ROWS_LOC) * COLS, COLS), :]

    for buf in (y0, y2):
        for j in range(N_PRE + 1):
            buf[pl.ds(j * PITCH, 8), :] = jnp.zeros((8, CH), f32)
    out_w = out_w_ref[...]
    out_w16 = out_w.astype(bf16)
    image = []
    for j in range(0, N_PRE, 2):
        lhs = jnp.concatenate([feats(j + k) for k in range(4)], axis=1)
        for b, buf in enumerate((y0, y1, y2)):
            prod = dot(lhs, two_ref[b], 1, 0)
            buf[pl.ds(j * PITCH + 8, COLS), :] = prod[:, :CH]
            buf[pl.ds((j + 1) * PITCH + 8, COLS), :] = prod[:, CH:]
    for j in range(N_PRE):
        at = j * PITCH + 8
        pre = y0[pl.ds(at - 1, COLS), :] + y1[pl.ds(at, COLS), :] + y2[pl.ds(at + 1, COLS), :]
        sig = sigmoid(pre)
        act = (pre * sig).astype(bf16)
        seen = dot(out_w16, act, 1, 1)
        if 2 <= j < 2 + ROWS_LOC:
            slope[j - 2] = sig * (1.0 + pre * (1.0 - sig))
            hidden[j - 2] = act
        else:
            seen = seen * valid(j - 2)
        image.append(seen)
    for j in range(ROWS_LOC):
        for c in range(3):
            recon_ref[c, j : j + 1, :] = image[j + 2][c : c + 1, :]
    image = jnp.concatenate(image, axis=0)

    truth[...] = jnp.zeros_like(truth)
    for k, ref in ((-1, up_ref), (1, down_ref)):
        rows = ref[pl.ds(SLAB, 32), :].astype(f32)
        for y in range(2):
            row, j = (y + 2, y) if k < 0 else (y, y + 6)
            for c in range(3):
                for h in range(COLS // CH):
                    at = (c * 2 + h) * ROWS_LOC + row
                    truth[j * 8 + c : j * 8 + c + 1, h * CH : (h + 1) * CH] = rows[at : at + 1]
    for y in range(ROWS_LOC):
        for c in range(3):
            at = (y + 2) * 8 + c
            truth[at : at + 1, :] = truth_ref[c, y : y + 1, :]
    true_image = truth[...]

    def taps(x):
        pad = jnp.zeros((K_BAND - 3 * N_PRE * 8, COLS), f32)
        return jnp.concatenate([shifted(x, 1), x, shifted(x, -1), pad], axis=0).astype(bf16)

    taps_a, taps_b = taps(image), taps(true_image)
    half = CH // 2

    def gelu(x):
        sq = x * x
        th = jnp.tanh(x * (GELU_K + (GELU_K * GELU_C) * sq))
        rise = 1.0 + th
        return x * rise, rise, th, sq

    def norm(twice):
        mean = jnp.sum(twice * twice, axis=0, keepdims=True) * (1.0 / half)
        return lax.rsqrt(mean + 4.0 * NORM_EPS)

    for r in range(N_LOSS):
        inside = 1 <= r < 1 + ROWS_LOC
        ok = 1.0 if inside else valid(r - 1)
        both = dot(band_ref[r * CH : (r + 1) * CH, :], taps_a, 1, 0)
        other = dot(band_ref[r * CH + half : (r + 1) * CH, :], taps_b, 1, 0)
        for side in range(2):
            cols = slice(side * CH, (side + 1) * CH)
            g, a, t = both[:half, cols], both[half:, cols], other[:, cols]
            head = heads_ref[:half, :] if inside else heads_ref[:half, :] * ok
            d_disc = head * (1.5 + jnp.tanh(g))
            fa, rise, th, sq = gelu(a)
            fb = gelu(t)[0]
            inv_a, inv_b = norm(fa), norm(fb)
            na = fa * inv_a
            up = heads_ref[half:, :] * (na - fb * inv_b)
            mean = jnp.sum(up * na, axis=0, keepdims=True) * (1.0 / half)
            d_feat = (inv_a * ok) * (up - na * mean)
            slant = rise + fa * (1.0 - th) * (GELU_K + (3.0 * GELU_K * GELU_C) * sq)
            dall[r * CH : r * CH + half, cols] = d_disc.astype(bf16)
            dall[r * CH + half : (r + 1) * CH, cols] = (d_feat * slant).astype(bf16)

    back = dot(band_t_ref[...], dall[...], 1, 0)
    n = N_GRAD * 8
    diff = (image - true_image)[16 : 16 + n]
    grad_image = (
        shifted(back[:n], -1) + back[n : 2 * n] + shifted(back[2 * n :], 1)
        + diff * lax.rsqrt(diff * diff + CHARB_EPS)
    )
    out_w2 = jnp.concatenate([out_w, out_w], axis=0).astype(bf16)
    grad_out = jnp.zeros((16, CH), f32)
    for q in range(N_GRAD):
        g = grad_image[q * 8 : (q + 1) * 8]
        high = g.astype(bf16).astype(f32)
        pair = jnp.concatenate([high, g - high], axis=0)
        grad_pre = dot(pair.T.astype(bf16), out_w2, 1, 0) * slope[q]
        grad_pre_ref[q] = grad_pre.astype(bf16)
        y0[pl.ds(q * PITCH + 8, COLS), :] = grad_pre
        grad_out = grad_out + dot(pair.astype(bf16), hidden[q], 1, 0)
    grad_out = grad_out[:8] + grad_out[8:]

    @pl.when(first)
    def _():
        far_edge_ref[...] = grad_pre_ref[0]
        near_edge_ref[...] = grad_pre_ref[ROWS_LOC - 1]

    @pl.when(jnp.logical_not(first))
    def _():
        near_edge_ref[...] = grad_pre_ref[0]
        far_edge_ref[...] = grad_pre_ref[ROWS_LOC - 1]

    lhs, rhs = [], []
    for y in range(ROWS_LOC):
        at = y * PITCH + 8
        lhs.append(
            jnp.concatenate([y0[pl.ds(at + 1 - b, COLS), :] for b in range(3)], axis=1).astype(bf16)
        )
        rhs.append(jnp.concatenate([feats(2 + y + a) for a in range(3)], axis=1))
    lhs, rhs = jnp.concatenate(lhs, axis=0), jnp.concatenate(rhs, axis=0)
    for k in range(64):
        packed[pl.ds(k * BLOCK + 18, 2), :] = jnp.zeros((2, CH), f32)
    for b in range(3):
        grad = dot(lhs[:, b * CH : (b + 1) * CH], rhs, 0, 0)
        for a in range(3):
            tap = a * 3 + b
            for d in range(8):
                block = grad[d * 16 : (d + 1) * 16, a * CH : (a + 1) * CH]
                start = tap * 16
                while start < tap * 16 + 16:
                    part, inner = divmod(start, 18)
                    count = min(18 - inner, tap * 16 + 16 - start)
                    at = ((d // 2) * 8 + part) * 2 * BLOCK + (d % 2) * BLOCK + inner
                    packed[pl.ds(at, count), :] = block[start - tap * 16 : start - tap * 16 + count]
                    start += count
    for d in range(8):
        for c in range(3):
            line = grad_out[c : c + 1]
            if d:
                line = pltpu.roll(line, CH - 16 * d, 1)
            packed[pl.ds(((d // 2) * 8 + c) * 2 * BLOCK + (d % 2) * BLOCK + 18, 1), :] = line
    piece_ref[...] = packed[...].astype(bf16)


def back_kernel(tile_ref, grad_ref, far_ref, near_ref, conv_ref, out_ref, z0, z1, z2, wide_ref):
    bf16, f32 = jnp.bfloat16, jnp.float32
    first = lax.rem(tile_ref[0], 2) == 0
    wide_ref[1 : 1 + ROWS_LOC] = grad_ref[...]

    @pl.when(first)
    def _():
        wide_ref[0] = far_ref[...]
        wide_ref[ROWS_LOC + 1] = near_ref[...]

    @pl.when(jnp.logical_not(first))
    def _():
        wide_ref[0] = near_ref[...]
        wide_ref[ROWS_LOC + 1] = far_ref[...]

    for buf in (z0, z2):
        for y in range(ROWS_LOC + 1):
            buf[pl.ds(y * PITCH, 8), :] = jnp.zeros((8, CH), f32)
    weights = jnp.concatenate(
        [jnp.concatenate([conv_ref[a, b] for a in range(3)], axis=1) for b in range(3)], axis=0
    )
    for y in range(ROWS_LOC):
        lhs = jnp.concatenate([wide_ref[y + 2 - a] for a in range(3)], axis=1)
        prod = dot(lhs, weights, 1, 1)
        for b, buf in enumerate((z0, z1, z2)):
            buf[pl.ds(y * PITCH + 8, COLS), :] = prod[:, b * CH : (b + 1) * CH]
    for y in range(ROWS_LOC):
        at = y * PITCH + 8
        total = z0[pl.ds(at + 1, COLS), :] + z1[pl.ds(at, COLS), :] + z2[pl.ds(at - 1, COLS), :]
        out_ref[y] = total.astype(bf16)


def first_sum_kernel(in_ref, out_ref):
    total = in_ref[0].astype(jnp.float32)
    for k in range(1, in_ref.shape[0]):
        total = total + in_ref[k].astype(jnp.float32)
    pad = jnp.zeros((PADDED - BLOCK, CH), jnp.float32)
    for half in range(2):
        part = jnp.concatenate([total[half * BLOCK : (half + 1) * BLOCK], pad], axis=0)
        for k in range(8):
            out_ref[half * 8 + k] = part.astype(jnp.bfloat16)


def second_sum_kernel(in_ref, out_ref):
    total = in_ref[0].astype(jnp.float32)
    for k in range(1, in_ref.shape[0]):
        total = total + in_ref[k].astype(jnp.float32)
    for k in range(8):
        out_ref[k] = total


def last_kernel(in_ref, conv_ref, out_ref):
    for k in range(8):
        conv_ref[pl.ds(k * 18, 18), :] = in_ref[k, 0:18, :]
    for c in range(3):
        out_ref[c : c + 1, :] = in_ref[c, 18:19, :16]


def call(kernel, out_shape, scratch=(), smem=0, whole=0, n_in=1, flops=0, vmem=4):
    specs = [pl.BlockSpec(memory_space=pltpu.SMEM)] * smem
    specs += [pl.BlockSpec(memory_space=pltpu.HBM)] * whole
    specs += [pl.BlockSpec(memory_space=VMEM)] * (n_in - smem - whole)
    many = isinstance(out_shape, tuple)
    return pl.pallas_call(
        kernel,
        out_shape=out_shape,
        in_specs=specs,
        out_specs=tuple(pl.BlockSpec(memory_space=VMEM) for _ in out_shape)
        if many
        else pl.BlockSpec(memory_space=VMEM),
        scratch_shapes=list(scratch),
        cost_estimate=pl.CostEstimate(flops=flops, bytes_accessed=1 << 20, transcendentals=0),
        compiler_params=pltpu.CompilerParams(vmem_limit_bytes=vmem << 20),
    )


def shape(*dims, dtype=jnp.float32):
    return jax.ShapeDtypeStruct(dims, dtype)


def pack(tile, features, targets):
    out = shape(SLAB + 32, CH, dtype=jnp.bfloat16)
    return call(
        pack_kernel,
        (out, out),
        scratch=[VMEM((3, ROWS_LOC, COLS), jnp.float32), pltpu.SemaphoreType.DMA((3,))],
        smem=1,
        n_in=3,
        whole=2,
    )(
        tile,
        pltpu.with_memory_space_constraint(features, pltpu.HBM),
        pltpu.with_memory_space_constraint(targets, pltpu.HBM),
    )


def prepare(conv_weight, disc_weight, disc_head, lpips_weight, lpips_lin, out_weight):
    bf16 = jnp.bfloat16
    return call(
        prep_kernel,
        (
            shape(N_LOSS * CH, K_BAND, dtype=bf16),
            shape(3 * N_GRAD * 8, N_LOSS * CH, dtype=bf16),
            shape(CH, CH),
            shape(8, CH),
            shape(3, 4 * CH, 2 * CH, dtype=bf16),
        ),
        scratch=[VMEM((32, CH), jnp.float32)],
        n_in=6,
        flops=1 << 28,
    )(
        disc_weight, lpips_weight, disc_head.reshape(1, -1), lpips_lin.reshape(1, -1),
        out_weight.T, conv_weight,
    )


def tile_step(tile, far, own, truth, near, band, band_t, heads, out_w, two):
    f32, bf16 = jnp.float32, jnp.bfloat16
    rows = N_PRE * PITCH + 8
    return call(
        main_kernel,
        (
            shape(3, ROWS_LOC, COLS),
            shape(ROWS_LOC, COLS, CH, dtype=bf16),
            shape(COLS, CH, dtype=bf16),
            shape(COLS, CH, dtype=bf16),
            shape(32 * 2 * BLOCK, CH, dtype=bf16),
        ),
        scratch=[
            VMEM((rows, CH), f32),
            VMEM((rows, CH), f32),
            VMEM((rows, CH), f32),
            VMEM((N_GRAD, COLS, CH), f32),
            VMEM((ROWS_LOC, COLS, CH), bf16),
            VMEM((N_PRE * 8, COLS), f32),
            VMEM((N_LOSS * CH, COLS), bf16),
            VMEM((32 * 2 * BLOCK, CH), f32),
            VMEM((SLAB + 32, CH), bf16),
            VMEM((SLAB + 32, CH), bf16),
        ],
        smem=1,
        n_in=10,
        flops=1 << 31,
        vmem=20,
    )(tile, far, own, truth, near, two, out_w, band, band_t, heads)


def back_step(tile, grad_pre, far, near, conv_weight):
    rows = ROWS_LOC * PITCH + 8
    return call(
        back_kernel,
        shape(ROWS_LOC, COLS, CH, dtype=jnp.bfloat16),
        scratch=[VMEM((rows, CH), jnp.float32)] * 3
        + [VMEM((ROWS_LOC + 2, COLS, CH), jnp.bfloat16)],
        smem=1,
        n_in=5,
        flops=1 << 30,
        vmem=8,
    )(tile, grad_pre, far, near, conv_weight)


def swap(array, axes):
    return lax.all_to_all(array, axes, split_axis=0, concat_axis=0, tiled=True)


def swaps(firsts):
    return [pair for i in firsts for pair in ((i, i + 1), (i + 1, i))]


ROWS = ("zl", "x", "core")


def body(
    features, conv_weight, out_weight, targets, disc_weight, disc_head, lpips_weight, lpips_lin
):
    tile = lax.axis_index(ROWS).astype(jnp.int32).reshape(1)
    own, truth = features[0].reshape(TILE, CH), jnp.transpose(targets[0], (2, 0, 1))
    on_chip, off_chip = swaps(range(0, TILES, 2)), swaps(range(1, TILES - 1, 2))
    near, far = pack(tile, own, truth)
    near, far = lax.ppermute(near, ROWS, on_chip), lax.ppermute(far, ROWS, off_chip)
    tables = prepare(
        conv_weight, disc_weight, disc_head, lpips_weight, lpips_lin, out_weight
    )
    recon, grad_pre, near, far, pieces = tile_step(tile, far, own, truth, near, *tables)
    pieces = swap(pieces.reshape(32, 2 * BLOCK, CH), ("y", "x", "core"))
    pieces = call(first_sum_kernel, shape(16, PADDED, CH, dtype=jnp.bfloat16))(pieces)
    pieces, near, far = lax.optimization_barrier((pieces, near, far))
    pieces = swap(pieces, ("zh", "zl"))
    near, far = lax.ppermute(near, ROWS, on_chip), lax.ppermute(far, ROWS, off_chip)
    grad_features = back_step(tile, grad_pre, far, near, conv_weight)
    pieces, grad_features = lax.optimization_barrier((pieces, grad_features))
    pieces = call(second_sum_kernel, shape(8, PADDED, CH))(pieces)
    pieces = swap(pieces, ("x", "core"))
    grad_conv, grad_out = call(last_kernel, (shape(144, CH), shape(3, 16)))(pieces)
    return (
        jnp.transpose(recon, (1, 2, 0))[None],
        grad_features[None],
        jnp.transpose(grad_conv.reshape(3, 3, 16, CH), (0, 1, 3, 2)),
        grad_out.T,
    )


def solution(mesh):
    fine = Mesh(mesh.devices.reshape(4, 2, 8, 4, 2), ("y", "zh", "zl", "x", "core"))
    dp = ("y", "zh")
    in_specs = (
        P(dp, ROWS, None, None), P(), P(), P(dp, ROWS, None, None), P(), P(), P(), P(),
    )
    out_specs = (
        P(dp, ROWS, None, None), P(dp, ROWS, None, None), P(None, None, None, dp), P(dp, None),
    )
    return jax.shard_map(body, mesh=fine, in_specs=in_specs, out_specs=out_specs, check_vma=False)
```

```python
import jax
import jax.numpy as jnp
from jax import lax
from jax.experimental import pallas as pl
from jax.experimental.pallas import tpu as pltpu
from jax.sharding import Mesh, PartitionSpec as P

ADV_SCALE = 0.5
CHARB_EPS = 0.01
NORM_EPS = 1e-06
GELU_K = 0.7978845608028654
GELU_C = 0.044715

ROWS_LOC = 4
COLS = 256
TILE = ROWS_LOC * COLS
CH = 128
TILES = 64
HEIGHT = ROWS_LOC * TILES
HALO = 3
SLAB = HALO * COLS
N_PRE = 8
N_LOSS = 6
N_GRAD = 4
PITCH = COLS + 8
K_BAND = 256
BLOCK = 20
PADDED = 24
VMEM = pltpu.VMEM


def select_ahead(r):
    lane = lax.broadcasted_iota(jnp.int32, (32, K_BAND), 1)
    b, j, c = lane // (N_PRE * 8), (lane // 8) % N_PRE, lane % 8
    return chosen(lax.broadcasted_iota(jnp.int32, (32, K_BAND), 0), j - r, b, c)


def select_back(r):
    dims = (3 * N_GRAD * 8, 32)
    line = lax.broadcasted_iota(jnp.int32, dims, 0)
    b, q, c = line // (N_GRAD * 8), (line // 8) % N_GRAD, line % 8
    return chosen(lax.broadcasted_iota(jnp.int32, dims, 1), q + 2 - r, b, c)


def chosen(tap, a, b, c):
    real = jnp.logical_and(jnp.logical_and(a >= 0, a < 3), jnp.logical_and(b < 3, c < 3))
    hit = jnp.logical_and(real, tap == 9 * a + 3 * b + c)
    return jnp.where(hit, 1.0, 0.0).astype(jnp.bfloat16)


def dot(a, b, ca, cb):
    return lax.dot_general(a, b, (((ca,), (cb,)), ((), ())), preferred_element_type=jnp.float32)


def sigmoid(x):
    return 1.0 / (1.0 + jnp.exp(-jnp.maximum(x, -87.0)))


def shifted(x, by):
    lane = lax.broadcasted_iota(jnp.int32, x.shape, 1)
    if by == 1:
        return jnp.where(lane == 0, 0.0, pltpu.roll(x, 1, 1))
    return jnp.where(lane == COLS - 1, 0.0, pltpu.roll(x, COLS - 1, 1))


def pack_kernel(tile_ref, own_ref, truth_ref, near_ref, far_ref, truth_vmem, sems):
    first = lax.rem(tile_ref[0], 2) == 0
    fetch = pltpu.make_async_copy(truth_ref, truth_vmem, sems.at[2])
    fetch.start()

    def slabs(top_ref, bottom_ref):
        top = pltpu.make_async_copy(
            own_ref.at[pl.ds(0, SLAB)], top_ref.at[pl.ds(0, SLAB)], sems.at[0]
        )
        bottom = pltpu.make_async_copy(
            own_ref.at[pl.ds(COLS, SLAB)], bottom_ref.at[pl.ds(0, SLAB)], sems.at[1]
        )
        top.start()
        bottom.start()
        fetch.wait()
        rows = [
            truth_vmem[c, :, h * CH : (h + 1) * CH] for c in range(3) for h in range(COLS // CH)
        ] + [jnp.zeros((8, CH), jnp.float32)]
        high = jnp.concatenate(rows, axis=0).astype(jnp.bfloat16)
        near_ref[pl.ds(SLAB, 32), :] = high
        far_ref[pl.ds(SLAB, 32), :] = high
        top.wait()
        bottom.wait()

    @pl.when(first)
    def _():
        slabs(far_ref, near_ref)

    @pl.when(jnp.logical_not(first))
    def _():
        slabs(near_ref, far_ref)


def prep_kernel(
    disc_ref, lpips_ref, head_ref, lin_ref, out_w_ref, conv_ref,
    band_ref, band_t_ref, heads_ref, wide_ref, two_ref, w27_ref,
):
    w27_ref[...] = jnp.zeros_like(w27_ref)
    for a in range(3):
        for b in range(3):
            pair = jnp.concatenate([disc_ref[a, b], lpips_ref[a, b]], axis=1)
            w27_ref[pl.ds((a * 3 + b) * 3, 3), :] = pair
    w27 = w27_ref[...].astype(jnp.bfloat16)
    for r in range(N_LOSS):
        band = dot(w27, select_ahead(r), 0, 0)
        band_ref[r * CH : r * CH + CH // 2, :] = (0.5 * band[: CH // 2]).astype(jnp.bfloat16)
        band_ref[r * CH + CH // 2 : (r + 1) * CH, :] = band[CH // 2 :].astype(jnp.bfloat16)
        back = dot(select_back(r), w27, 1, 0)
        band_t_ref[:, r * CH : (r + 1) * CH] = back.astype(jnp.bfloat16)
    line = jnp.concatenate([-0.4 * ADV_SCALE * head_ref[...], 2.0 * lin_ref[...]], axis=1)
    heads_ref[...] = jnp.broadcast_to(line, (CH, CH)).T
    wide_ref[...] = jnp.zeros_like(wide_ref)
    wide_ref[0:3, :] = out_w_ref[...].astype(jnp.float32)
    zero = jnp.zeros((CH, CH), jnp.bfloat16)
    for b in range(3):
        for k in range(4):
            two_ref[b, k * CH : (k + 1) * CH, :CH] = conv_ref[k, b] if k < 3 else zero
            two_ref[b, k * CH : (k + 1) * CH, CH:] = conv_ref[k - 1, b] if k else zero


def main_kernel(
    tile_ref, far_ref, own_ref, truth_ref, near_ref, two_ref, out_w_ref,
    band_ref, band_t_ref, heads_ref,
    recon_ref, grad_pre_ref, near_edge_ref, far_edge_ref, piece_ref,
    y0, y1, y2, slope, hidden, truth, dall, packed, up_ref, down_ref,
):
    bf16, f32 = jnp.bfloat16, jnp.float32

    first = lax.rem(tile_ref[0], 2) == 0

    @pl.when(first)
    def _():
        up_ref[...] = far_ref[...]
        down_ref[...] = near_ref[...]

    @pl.when(jnp.logical_not(first))
    def _():
        up_ref[...] = near_ref[...]
        down_ref[...] = far_ref[...]

    first_row = tile_ref[0] * ROWS_LOC

    def valid(row):
        inside = jnp.logical_and(first_row + row >= 0, first_row + row < HEIGHT)
        return jnp.where(inside, 1.0, 0.0).astype(f32)

    def feats(j):
        if j < HALO:
            return up_ref[pl.ds(j * COLS, COLS), :]
        if j < HALO + ROWS_LOC:
            return own_ref[pl.ds((j - HALO) * COLS, COLS), :]
        return down_ref[pl.ds((j - HALO - ROWS_LOC) * COLS, COLS), :]

    for buf in (y0, y2):
        for j in range(N_PRE + 1):
            buf[pl.ds(j * PITCH, 8), :] = jnp.zeros((8, CH), f32)
    out_w = out_w_ref[...]
    out_w16 = out_w.astype(bf16)
    image = []
    for j in range(0, N_PRE, 2):
        lhs = jnp.concatenate([feats(j + k) for k in range(4)], axis=1)
        for b, buf in enumerate((y0, y1, y2)):
            prod = dot(lhs, two_ref[b], 1, 0)
            buf[pl.ds(j * PITCH + 8, COLS), :] = prod[:, :CH]
            buf[pl.ds((j + 1) * PITCH + 8, COLS), :] = prod[:, CH:]
    for j in range(N_PRE):
        at = j * PITCH + 8
        pre = y0[pl.ds(at - 1, COLS), :] + y1[pl.ds(at, COLS), :] + y2[pl.ds(at + 1, COLS), :]
        sig = sigmoid(pre)
        act = (pre * sig).astype(bf16)
        seen = dot(out_w16, act, 1, 1)
        if 2 <= j < 2 + ROWS_LOC:
            slope[j - 2] = sig * (1.0 + pre * (1.0 - sig))
            hidden[j - 2] = act
        else:
            seen = seen * valid(j - 2)
        image.append(seen)
    for j in range(ROWS_LOC):
        for c in range(3):
            recon_ref[c, j : j + 1, :] = image[j + 2][c : c + 1, :]
    image = jnp.concatenate(image, axis=0)

    truth[...] = jnp.zeros_like(truth)
    for k, ref in ((-1, up_ref), (1, down_ref)):
        rows = ref[pl.ds(SLAB, 32), :].astype(f32)
        for y in range(2):
            row, j = (y + 2, y) if k < 0 else (y, y + 6)
            for c in range(3):
                for h in range(COLS // CH):
                    at = (c * 2 + h) * ROWS_LOC + row
                    truth[j * 8 + c : j * 8 + c + 1, h * CH : (h + 1) * CH] = rows[at : at + 1]
    for y in range(ROWS_LOC):
        for c in range(3):
            at = (y + 2) * 8 + c
            truth[at : at + 1, :] = truth_ref[c, y : y + 1, :]
    true_image = truth[...]

    def taps(x):
        pad = jnp.zeros((K_BAND - 3 * N_PRE * 8, COLS), f32)
        return jnp.concatenate([shifted(x, 1), x, shifted(x, -1), pad], axis=0).astype(bf16)

    taps_a, taps_b = taps(image), taps(true_image)
    half = CH // 2

    def gelu(x):
        sq = x * x
        th = jnp.tanh(x * (GELU_K + (GELU_K * GELU_C) * sq))
        rise = 1.0 + th
        return x * rise, rise, th, sq

    def norm(twice):
        mean = jnp.sum(twice * twice, axis=0, keepdims=True) * (1.0 / half)
        return lax.rsqrt(mean + 4.0 * NORM_EPS)

    for r in range(N_LOSS):
        inside = 1 <= r < 1 + ROWS_LOC
        ok = 1.0 if inside else valid(r - 1)
        both = dot(band_ref[r * CH : (r + 1) * CH, :], taps_a, 1, 0)
        other = dot(band_ref[r * CH + half : (r + 1) * CH, :], taps_b, 1, 0)
        for side in range(2):
            cols = slice(side * CH, (side + 1) * CH)
            g, a, t = both[:half, cols], both[half:, cols], other[:, cols]
            head = heads_ref[:half, :] if inside else heads_ref[:half, :] * ok
            d_disc = head * (1.5 + jnp.tanh(g))
            fa, rise, th, sq = gelu(a)
            fb = gelu(t)[0]
            inv_a, inv_b = norm(fa), norm(fb)
            na = fa * inv_a
            up = heads_ref[half:, :] * (na - fb * inv_b)
            mean = jnp.sum(up * na, axis=0, keepdims=True) * (1.0 / half)
            d_feat = (inv_a * ok) * (up - na * mean)
            slant = rise + fa * (1.0 - th) * (GELU_K + (3.0 * GELU_K * GELU_C) * sq)
            dall[r * CH : r * CH + half, cols] = d_disc.astype(bf16)
            dall[r * CH + half : (r + 1) * CH, cols] = (d_feat * slant).astype(bf16)

    back = dot(band_t_ref[...], dall[...], 1, 0)
    n = N_GRAD * 8
    diff = (image - true_image)[16 : 16 + n]
    grad_image = (
        shifted(back[:n], -1) + back[n : 2 * n] + shifted(back[2 * n :], 1)
        + diff * lax.rsqrt(diff * diff + CHARB_EPS)
    )
    out_w2 = jnp.concatenate([out_w, out_w], axis=0).astype(bf16)
    grad_out = jnp.zeros((16, CH), f32)
    for q in range(N_GRAD):
        g = grad_image[q * 8 : (q + 1) * 8]
        high = g.astype(bf16).astype(f32)
        pair = jnp.concatenate([high, g - high], axis=0)
        grad_pre = dot(pair.T.astype(bf16), out_w2, 1, 0) * slope[q]
        grad_pre_ref[q] = grad_pre.astype(bf16)
        y0[pl.ds(q * PITCH + 8, COLS), :] = grad_pre
        grad_out = grad_out + dot(pair.astype(bf16), hidden[q], 1, 0)
    grad_out = grad_out[:8] + grad_out[8:]

    edge = jnp.where(first, 0, ROWS_LOC - 1)
    far_edge_ref[...] = grad_pre_ref[edge]
    near_edge_ref[...] = grad_pre_ref[ROWS_LOC - 1 - edge]

    lhs, rhs = [], []
    for y in range(ROWS_LOC):
        at = y * PITCH + 8
        lhs.append(
            jnp.concatenate([y0[pl.ds(at + 1 - b, COLS), :] for b in range(3)], axis=1).astype(bf16)
        )
        rhs.append(jnp.concatenate([feats(2 + y + a) for a in range(3)], axis=1))
    lhs, rhs = jnp.concatenate(lhs, axis=0), jnp.concatenate(rhs, axis=0)
    for k in range(64):
        packed[pl.ds(k * BLOCK + 18, 2), :] = jnp.zeros((2, CH), f32)
    for b in range(3):
        grad = dot(lhs[:, b * CH : (b + 1) * CH], rhs, 0, 0)
        for a in range(3):
            tap = a * 3 + b
            for d in range(8):
                block = grad[d * 16 : (d + 1) * 16, a * CH : (a + 1) * CH]
                start = tap * 16
                while start < tap * 16 + 16:
                    part, inner = divmod(start, 18)
                    count = min(18 - inner, tap * 16 + 16 - start)
                    at = ((d // 2) * 8 + part) * 2 * BLOCK + (d % 2) * BLOCK + inner
                    packed[pl.ds(at, count), :] = block[start - tap * 16 : start - tap * 16 + count]
                    start += count
    for d in range(8):
        for c in range(3):
            line = grad_out[c : c + 1]
            if d:
                line = pltpu.roll(line, CH - 16 * d, 1)
            packed[pl.ds(((d // 2) * 8 + c) * 2 * BLOCK + (d % 2) * BLOCK + 18, 1), :] = line
    piece_ref[...] = packed[...].astype(bf16)


def back_kernel(
    tile_ref, grad_ref, far_ref, near_ref, conv_ref, recon_ref,
    out_ref, recon_out_ref, z0, z1, z2, wide_ref,
):
    bf16, f32 = jnp.bfloat16, jnp.float32
    recon_out_ref[...] = recon_ref[...]
    first = lax.rem(tile_ref[0], 2) == 0
    wide_ref[1 : 1 + ROWS_LOC] = grad_ref[...]

    @pl.when(first)
    def _():
        wide_ref[0] = far_ref[...]
        wide_ref[ROWS_LOC + 1] = near_ref[...]

    @pl.when(jnp.logical_not(first))
    def _():
        wide_ref[0] = near_ref[...]
        wide_ref[ROWS_LOC + 1] = far_ref[...]

    for buf in (z0, z2):
        for y in range(ROWS_LOC + 1):
            buf[pl.ds(y * PITCH, 8), :] = jnp.zeros((8, CH), f32)
    weights = jnp.concatenate(
        [jnp.concatenate([conv_ref[a, b] for a in range(3)], axis=1) for b in range(3)], axis=0
    )
    for y in range(ROWS_LOC):
        lhs = jnp.concatenate([wide_ref[y + 2 - a] for a in range(3)], axis=1)
        prod = dot(lhs, weights, 1, 1)
        for b, buf in enumerate((z0, z1, z2)):
            buf[pl.ds(y * PITCH + 8, COLS), :] = prod[:, b * CH : (b + 1) * CH]
    for y in range(ROWS_LOC):
        at = y * PITCH + 8
        total = z0[pl.ds(at + 1, COLS), :] + z1[pl.ds(at, COLS), :] + z2[pl.ds(at - 1, COLS), :]
        out_ref[y] = total.astype(bf16)


def first_sum_kernel(in_ref, out_ref):
    total = in_ref[0].astype(jnp.float32)
    for k in range(1, in_ref.shape[0]):
        total = total + in_ref[k].astype(jnp.float32)
    pad = jnp.zeros((PADDED - BLOCK, CH), jnp.float32)
    for half in range(2):
        part = jnp.concatenate([total[half * BLOCK : (half + 1) * BLOCK], pad], axis=0)
        for k in range(8):
            out_ref[half * 8 + k] = part.astype(jnp.bfloat16)


def second_sum_kernel(in_ref, out_ref):
    total = in_ref[0].astype(jnp.float32)
    for k in range(1, in_ref.shape[0]):
        total = total + in_ref[k].astype(jnp.float32)
    for k in range(8):
        out_ref[k] = total


def last_kernel(in_ref, conv_ref, out_ref):
    for k in range(8):
        conv_ref[pl.ds(k * 18, 18), :] = in_ref[k, 0:18, :]
    for c in range(3):
        out_ref[c : c + 1, :] = in_ref[c, 18:19, :16]


def call(kernel, out_shape, scratch=(), smem=0, whole=0, n_in=1, flops=0, vmem=4):
    specs = [pl.BlockSpec(memory_space=pltpu.SMEM)] * smem
    specs += [pl.BlockSpec(memory_space=pltpu.HBM)] * whole
    specs += [pl.BlockSpec(memory_space=VMEM)] * (n_in - smem - whole)
    many = isinstance(out_shape, tuple)
    return pl.pallas_call(
        kernel,
        out_shape=out_shape,
        in_specs=specs,
        out_specs=tuple(pl.BlockSpec(memory_space=VMEM) for _ in out_shape)
        if many
        else pl.BlockSpec(memory_space=VMEM),
        scratch_shapes=list(scratch),
        cost_estimate=pl.CostEstimate(flops=flops, bytes_accessed=1 << 20, transcendentals=0),
        compiler_params=pltpu.CompilerParams(vmem_limit_bytes=vmem << 20),
    )


def shape(*dims, dtype=jnp.float32):
    return jax.ShapeDtypeStruct(dims, dtype)


def pack(tile, features, targets):
    out = shape(SLAB + 32, CH, dtype=jnp.bfloat16)
    return call(
        pack_kernel,
        (out, out),
        scratch=[VMEM((3, ROWS_LOC, COLS), jnp.float32), pltpu.SemaphoreType.DMA((3,))],
        smem=1,
        n_in=3,
        whole=2,
    )(
        tile,
        pltpu.with_memory_space_constraint(features, pltpu.HBM),
        pltpu.with_memory_space_constraint(targets, pltpu.HBM),
    )


def prepare(conv_weight, disc_weight, disc_head, lpips_weight, lpips_lin, out_weight):
    bf16 = jnp.bfloat16
    return call(
        prep_kernel,
        (
            shape(N_LOSS * CH, K_BAND, dtype=bf16),
            shape(3 * N_GRAD * 8, N_LOSS * CH, dtype=bf16),
            shape(CH, CH),
            shape(8, CH),
            shape(3, 4 * CH, 2 * CH, dtype=bf16),
        ),
        scratch=[VMEM((32, CH), jnp.float32)],
        n_in=6,
        flops=1 << 28,
    )(
        disc_weight, lpips_weight, disc_head.reshape(1, -1), lpips_lin.reshape(1, -1),
        out_weight.T, conv_weight,
    )


def tile_step(tile, far, own, truth, near, band, band_t, heads, out_w, two):
    f32, bf16 = jnp.float32, jnp.bfloat16
    rows = N_PRE * PITCH + 8
    return call(
        main_kernel,
        (
            shape(3, ROWS_LOC, COLS),
            shape(ROWS_LOC, COLS, CH, dtype=bf16),
            shape(COLS, CH, dtype=bf16),
            shape(COLS, CH, dtype=bf16),
            shape(32 * 2 * BLOCK, CH, dtype=bf16),
        ),
        scratch=[
            VMEM((rows, CH), f32),
            VMEM((rows, CH), f32),
            VMEM((rows, CH), f32),
            VMEM((N_GRAD, COLS, CH), f32),
            VMEM((ROWS_LOC, COLS, CH), bf16),
            VMEM((N_PRE * 8, COLS), f32),
            VMEM((N_LOSS * CH, COLS), bf16),
            VMEM((32 * 2 * BLOCK, CH), f32),
            VMEM((SLAB + 32, CH), bf16),
            VMEM((SLAB + 32, CH), bf16),
        ],
        smem=1,
        n_in=10,
        flops=1 << 31,
        vmem=20,
    )(tile, far, own, truth, near, two, out_w, band, band_t, heads)


def back_step(tile, grad_pre, far, near, conv_weight, recon):
    rows = ROWS_LOC * PITCH + 8
    return call(
        back_kernel,
        (shape(ROWS_LOC, COLS, CH, dtype=jnp.bfloat16), shape(3, ROWS_LOC, COLS)),
        scratch=[VMEM((rows, CH), jnp.float32)] * 3
        + [VMEM((ROWS_LOC + 2, COLS, CH), jnp.bfloat16)],
        smem=1,
        n_in=6,
        flops=1 << 30,
        vmem=8,
    )(tile, grad_pre, far, near, conv_weight, recon)


def swap(array, axes):
    return lax.all_to_all(array, axes, split_axis=0, concat_axis=0, tiled=True)


def swaps(firsts):
    return [pair for i in firsts for pair in ((i, i + 1), (i + 1, i))]


ROWS = ("zl", "x", "core")


def body(
    features, conv_weight, out_weight, targets, disc_weight, disc_head, lpips_weight, lpips_lin
):
    tile = lax.axis_index(ROWS).astype(jnp.int32).reshape(1)
    own, truth = features[0].reshape(TILE, CH), jnp.transpose(targets[0], (2, 0, 1))
    on_chip, off_chip = swaps(range(0, TILES, 2)), swaps(range(1, TILES - 1, 2))
    near, far = pack(tile, own, truth)
    near, far = lax.ppermute(near, ROWS, on_chip), lax.ppermute(far, ROWS, off_chip)
    tables = prepare(
        conv_weight, disc_weight, disc_head, lpips_weight, lpips_lin, out_weight
    )
    recon, grad_pre, near, far, pieces = tile_step(tile, far, own, truth, near, *tables)
    pieces = swap(pieces.reshape(32, 2 * BLOCK, CH), ("y", "x", "core"))
    pieces = call(first_sum_kernel, shape(16, PADDED, CH, dtype=jnp.bfloat16))(pieces)
    pieces, near, far = lax.optimization_barrier((pieces, near, far))
    pieces = swap(pieces, ("zh", "zl"))
    near, far = lax.ppermute(near, ROWS, on_chip), lax.ppermute(far, ROWS, off_chip)
    grad_features, recon = back_step(tile, grad_pre, far, near, conv_weight, recon)
    pieces, grad_features, recon = lax.optimization_barrier((pieces, grad_features, recon))
    pieces = call(second_sum_kernel, shape(8, PADDED, CH))(pieces)
    pieces = swap(pieces, ("x", "core"))
    grad_conv, grad_out = call(last_kernel, (shape(144, CH), shape(3, 16)))(pieces)
    return (
        jnp.transpose(recon, (1, 2, 0))[None],
        grad_features[None],
        jnp.transpose(grad_conv.reshape(3, 3, 16, CH), (0, 1, 3, 2)),
        grad_out.T,
    )


def solution(mesh):
    fine = Mesh(mesh.devices.reshape(4, 2, 8, 4, 2), ("y", "zh", "zl", "x", "core"))
    dp = ("y", "zh")
    in_specs = (
        P(dp, ROWS, None, None), P(), P(), P(dp, ROWS, None, None), P(), P(), P(), P(),
    )
    out_specs = (
        P(dp, ROWS, None, None), P(dp, ROWS, None, None), P(None, None, None, dp), P(dp, None),
    )
    return jax.shard_map(body, mesh=fine, in_specs=in_specs, out_specs=out_specs, check_vma=False)
```

```python
import jax
import jax.numpy as jnp
from jax import lax
from jax.experimental import pallas as pl
from jax.experimental.pallas import tpu as pltpu
from jax.sharding import Mesh, PartitionSpec as P

ADV_SCALE = 0.5
CHARB_EPS = 0.01
NORM_EPS = 1e-06
GELU_K = 0.7978845608028654
GELU_C = 0.044715

ROWS_LOC = 4
COLS = 256
TILE = ROWS_LOC * COLS
CH = 128
TILES = 64
HEIGHT = ROWS_LOC * TILES
HALO = 3
SLAB = HALO * COLS
N_PRE = 8
N_LOSS = 6
N_GRAD = 4
PITCH = COLS + 8
K_BAND = 256
BLOCK = 20
PADDED = 24
VMEM = pltpu.VMEM


def select_ahead(r):
    lane = lax.broadcasted_iota(jnp.int32, (32, K_BAND), 1)
    b, j, c = lane // (N_PRE * 8), (lane // 8) % N_PRE, lane % 8
    return chosen(lax.broadcasted_iota(jnp.int32, (32, K_BAND), 0), j - r, b, c)


def select_back(r):
    dims = (3 * N_GRAD * 8, 32)
    line = lax.broadcasted_iota(jnp.int32, dims, 0)
    b, q, c = line // (N_GRAD * 8), (line // 8) % N_GRAD, line % 8
    return chosen(lax.broadcasted_iota(jnp.int32, dims, 1), q + 2 - r, b, c)


def chosen(tap, a, b, c):
    real = jnp.logical_and(jnp.logical_and(a >= 0, a < 3), jnp.logical_and(b < 3, c < 3))
    hit = jnp.logical_and(real, tap == 9 * a + 3 * b + c)
    return jnp.where(hit, 1.0, 0.0).astype(jnp.bfloat16)


def dot(a, b, ca, cb):
    return lax.dot_general(a, b, (((ca,), (cb,)), ((), ())), preferred_element_type=jnp.float32)


def sigmoid(x):
    return 1.0 / (1.0 + jnp.exp(-jnp.maximum(x, -87.0)))


def shifted(x, by):
    lane = lax.broadcasted_iota(jnp.int32, x.shape, 1)
    if by == 1:
        return jnp.where(lane == 0, 0.0, pltpu.roll(x, 1, 1))
    return jnp.where(lane == COLS - 1, 0.0, pltpu.roll(x, COLS - 1, 1))


def pack_kernel(tile_ref, own_ref, truth_ref, near_ref, far_ref, truth_vmem, sems):
    first = lax.rem(tile_ref[0], 2) == 0
    fetch = pltpu.make_async_copy(truth_ref, truth_vmem, sems.at[2])
    fetch.start()

    def slabs(top_ref, bottom_ref):
        top = pltpu.make_async_copy(
            own_ref.at[pl.ds(0, SLAB)], top_ref.at[pl.ds(0, SLAB)], sems.at[0]
        )
        bottom = pltpu.make_async_copy(
            own_ref.at[pl.ds(COLS, SLAB)], bottom_ref.at[pl.ds(0, SLAB)], sems.at[1]
        )
        top.start()
        bottom.start()
        fetch.wait()
        rows = [
            truth_vmem[c, :, h * CH : (h + 1) * CH] for c in range(3) for h in range(COLS // CH)
        ] + [jnp.zeros((8, CH), jnp.float32)]
        high = jnp.concatenate(rows, axis=0).astype(jnp.bfloat16)
        near_ref[pl.ds(SLAB, 32), :] = high
        far_ref[pl.ds(SLAB, 32), :] = high
        top.wait()
        bottom.wait()

    @pl.when(first)
    def _():
        slabs(far_ref, near_ref)

    @pl.when(jnp.logical_not(first))
    def _():
        slabs(near_ref, far_ref)


def prep_kernel(
    disc_ref, lpips_ref, head_ref, lin_ref, out_w_ref, conv_ref,
    band_ref, band_t_ref, heads_ref, wide_ref, two_ref, w27_ref,
):
    w27_ref[...] = jnp.zeros_like(w27_ref)
    for a in range(3):
        for b in range(3):
            pair = jnp.concatenate([disc_ref[a, b], lpips_ref[a, b]], axis=1)
            w27_ref[pl.ds((a * 3 + b) * 3, 3), :] = pair
    w27 = w27_ref[...].astype(jnp.bfloat16)
    for r in range(N_LOSS):
        band = dot(w27, select_ahead(r), 0, 0)
        band_ref[r * CH : r * CH + CH // 2, :] = (0.5 * band[: CH // 2]).astype(jnp.bfloat16)
        band_ref[r * CH + CH // 2 : (r + 1) * CH, :] = band[CH // 2 :].astype(jnp.bfloat16)
        back = dot(select_back(r), w27, 1, 0)
        band_t_ref[:, r * CH : (r + 1) * CH] = back.astype(jnp.bfloat16)
    line = jnp.concatenate([-0.4 * ADV_SCALE * head_ref[...], 2.0 * lin_ref[...]], axis=1)
    heads_ref[...] = jnp.broadcast_to(line, (CH, CH)).T
    wide_ref[...] = jnp.zeros_like(wide_ref)
    wide_ref[0:3, :] = out_w_ref[...].astype(jnp.float32)
    zero = jnp.zeros((CH, CH), jnp.bfloat16)
    for b in range(3):
        for k in range(4):
            two_ref[b, k * CH : (k + 1) * CH, :CH] = conv_ref[k, b] if k < 3 else zero
            two_ref[b, k * CH : (k + 1) * CH, CH:] = conv_ref[k - 1, b] if k else zero


def main_kernel(
    tile_ref, far_ref, own_ref, truth_ref, near_ref, two_ref, out_w_ref,
    band_ref, band_t_ref, heads_ref,
    recon_ref, grad_pre_ref, near_edge_ref, far_edge_ref, piece_ref,
    y0, y1, y2, slope, hidden, truth, dall, packed, up_ref, down_ref,
):
    bf16, f32 = jnp.bfloat16, jnp.float32

    first = lax.rem(tile_ref[0], 2) == 0

    @pl.when(first)
    def _():
        up_ref[...] = far_ref[...]
        down_ref[...] = near_ref[...]

    @pl.when(jnp.logical_not(first))
    def _():
        up_ref[...] = near_ref[...]
        down_ref[...] = far_ref[...]

    first_row = tile_ref[0] * ROWS_LOC

    def valid(row):
        inside = jnp.logical_and(first_row + row >= 0, first_row + row < HEIGHT)
        return jnp.where(inside, 1.0, 0.0).astype(f32)

    def feats(j):
        if j < HALO:
            return up_ref[pl.ds(j * COLS, COLS), :]
        if j < HALO + ROWS_LOC:
            return own_ref[pl.ds((j - HALO) * COLS, COLS), :]
        return down_ref[pl.ds((j - HALO - ROWS_LOC) * COLS, COLS), :]

    for buf in (y0, y2):
        for j in range(N_PRE + 1):
            buf[pl.ds(j * PITCH, 8), :] = jnp.zeros((8, CH), f32)
    out_w = out_w_ref[...]
    out_w16 = out_w.astype(bf16)
    image = []
    for j in range(0, N_PRE, 2):
        lhs = jnp.concatenate([feats(j + k) for k in range(4)], axis=1)
        for b, buf in enumerate((y0, y1, y2)):
            prod = dot(lhs, two_ref[b], 1, 0)
            buf[pl.ds(j * PITCH + 8, COLS), :] = prod[:, :CH]
            buf[pl.ds((j + 1) * PITCH + 8, COLS), :] = prod[:, CH:]
    for j in range(N_PRE):
        at = j * PITCH + 8
        pre = y0[pl.ds(at - 1, COLS), :] + y1[pl.ds(at, COLS), :] + y2[pl.ds(at + 1, COLS), :]
        sig = sigmoid(pre)
        act = (pre * sig).astype(bf16)
        seen = dot(out_w16, act, 1, 1)
        if 2 <= j < 2 + ROWS_LOC:
            slope[j - 2] = sig * (1.0 + pre * (1.0 - sig))
            hidden[j - 2] = act
        else:
            seen = seen * valid(j - 2)
        image.append(seen)
    for j in range(ROWS_LOC):
        for c in range(3):
            recon_ref[c, j : j + 1, :] = image[j + 2][c : c + 1, :]
    image = jnp.concatenate(image, axis=0)

    truth[...] = jnp.zeros_like(truth)
    for k, ref in ((-1, up_ref), (1, down_ref)):
        rows = ref[pl.ds(SLAB, 32), :].astype(f32)
        for y in range(2):
            row, j = (y + 2, y) if k < 0 else (y, y + 6)
            for c in range(3):
                for h in range(COLS // CH):
                    at = (c * 2 + h) * ROWS_LOC + row
                    truth[j * 8 + c : j * 8 + c + 1, h * CH : (h + 1) * CH] = rows[at : at + 1]
    for y in range(ROWS_LOC):
        for c in range(3):
            at = (y + 2) * 8 + c
            truth[at : at + 1, :] = truth_ref[c, y : y + 1, :]
    true_image = truth[...]

    def taps(x):
        pad = jnp.zeros((K_BAND - 3 * N_PRE * 8, COLS), f32)
        return jnp.concatenate([shifted(x, 1), x, shifted(x, -1), pad], axis=0).astype(bf16)

    taps_a, taps_b = taps(image), taps(true_image)
    half = CH // 2

    def gelu(x):
        sq = x * x
        th = jnp.tanh(x * (GELU_K + (GELU_K * GELU_C) * sq))
        rise = 1.0 + th
        return x * rise, rise, th, sq

    def norm(twice):
        mean = jnp.sum(twice * twice, axis=0, keepdims=True) * (1.0 / half)
        return lax.rsqrt(mean + 4.0 * NORM_EPS)

    for r in range(N_LOSS):
        inside = 1 <= r < 1 + ROWS_LOC
        ok = 1.0 if inside else valid(r - 1)
        both = dot(band_ref[r * CH : (r + 1) * CH, :], taps_a, 1, 0)
        other = dot(band_ref[r * CH + half : (r + 1) * CH, :], taps_b, 1, 0)
        for side in range(2):
            cols = slice(side * CH, (side + 1) * CH)
            g, a, t = both[:half, cols], both[half:, cols], other[:, cols]
            head = heads_ref[:half, :] if inside else heads_ref[:half, :] * ok
            d_disc = head * (1.5 + jnp.tanh(g))
            fa, rise, th, sq = gelu(a)
            fb = gelu(t)[0]
            inv_a, inv_b = norm(fa), norm(fb)
            na = fa * inv_a
            up = heads_ref[half:, :] * (na - fb * inv_b)
            mean = jnp.sum(up * na, axis=0, keepdims=True) * (1.0 / half)
            d_feat = (inv_a * ok) * (up - na * mean)
            slant = rise + fa * (1.0 - th) * (GELU_K + (3.0 * GELU_K * GELU_C) * sq)
            dall[r * CH : r * CH + half, cols] = d_disc.astype(bf16)
            dall[r * CH + half : (r + 1) * CH, cols] = (d_feat * slant).astype(bf16)

    back = dot(band_t_ref[...], dall[...], 1, 0)
    n = N_GRAD * 8
    diff = (image - true_image)[16 : 16 + n]
    grad_image = (
        shifted(back[:n], -1) + back[n : 2 * n] + shifted(back[2 * n :], 1)
        + diff * lax.rsqrt(diff * diff + CHARB_EPS)
    )
    out_w2 = jnp.concatenate([out_w, out_w], axis=0).astype(bf16)
    grad_out = jnp.zeros((16, CH), f32)
    for q in range(N_GRAD):
        g = grad_image[q * 8 : (q + 1) * 8]
        high = g.astype(bf16).astype(f32)
        pair = jnp.concatenate([high, g - high], axis=0)
        grad_pre = dot(pair.T.astype(bf16), out_w2, 1, 0) * slope[q]
        grad_pre_ref[q] = grad_pre.astype(bf16)
        y0[pl.ds(q * PITCH + 8, COLS), :] = grad_pre
        grad_out = grad_out + dot(pair.astype(bf16), hidden[q], 1, 0)
    grad_out = grad_out[:8] + grad_out[8:]

    edge = jnp.where(first, 0, ROWS_LOC - 1)
    far_edge_ref[...] = grad_pre_ref[edge]
    near_edge_ref[...] = grad_pre_ref[ROWS_LOC - 1 - edge]

    lhs, rhs = [], []
    for y in range(ROWS_LOC):
        at = y * PITCH + 8
        lhs.append(
            jnp.concatenate([y0[pl.ds(at + 1 - b, COLS), :] for b in range(3)], axis=1).astype(bf16)
        )
        rhs.append(jnp.concatenate([feats(2 + y + a) for a in range(3)], axis=1))
    lhs, rhs = jnp.concatenate(lhs, axis=0), jnp.concatenate(rhs, axis=0)
    for k in range(64):
        packed[pl.ds(k * BLOCK + 18, 2), :] = jnp.zeros((2, CH), f32)
    for b in range(3):
        grad = dot(lhs[:, b * CH : (b + 1) * CH], rhs, 0, 0)
        for a in range(3):
            tap = a * 3 + b
            for d in range(8):
                block = grad[d * 16 : (d + 1) * 16, a * CH : (a + 1) * CH]
                start = tap * 16
                while start < tap * 16 + 16:
                    part, inner = divmod(start, 18)
                    count = min(18 - inner, tap * 16 + 16 - start)
                    at = (part * 4 + d // 2) * 2 * BLOCK + (d % 2) * BLOCK + inner
                    packed[pl.ds(at, count), :] = block[start - tap * 16 : start - tap * 16 + count]
                    start += count
    for d in range(8):
        for c in range(3):
            line = grad_out[c : c + 1]
            if d:
                line = pltpu.roll(line, CH - 16 * d, 1)
            packed[pl.ds((c * 4 + d // 2) * 2 * BLOCK + (d % 2) * BLOCK + 18, 1), :] = line
    piece_ref[...] = packed[...].astype(bf16)


def back_kernel(
    tile_ref, grad_ref, far_ref, near_ref, conv_ref, recon_ref,
    out_ref, recon_out_ref, z0, z1, z2, wide_ref,
):
    bf16, f32 = jnp.bfloat16, jnp.float32
    recon_out_ref[...] = recon_ref[...]
    first = lax.rem(tile_ref[0], 2) == 0
    wide_ref[1 : 1 + ROWS_LOC] = grad_ref[...]

    @pl.when(first)
    def _():
        wide_ref[0] = far_ref[...]
        wide_ref[ROWS_LOC + 1] = near_ref[...]

    @pl.when(jnp.logical_not(first))
    def _():
        wide_ref[0] = near_ref[...]
        wide_ref[ROWS_LOC + 1] = far_ref[...]

    for buf in (z0, z2):
        for y in range(ROWS_LOC + 1):
            buf[pl.ds(y * PITCH, 8), :] = jnp.zeros((8, CH), f32)
    weights = jnp.concatenate(
        [jnp.concatenate([conv_ref[a, b] for a in range(3)], axis=1) for b in range(3)], axis=0
    )
    for y in range(ROWS_LOC):
        lhs = jnp.concatenate([wide_ref[y + 2 - a] for a in range(3)], axis=1)
        prod = dot(lhs, weights, 1, 1)
        for b, buf in enumerate((z0, z1, z2)):
            buf[pl.ds(y * PITCH + 8, COLS), :] = prod[:, b * CH : (b + 1) * CH]
    for y in range(ROWS_LOC):
        at = y * PITCH + 8
        total = z0[pl.ds(at + 1, COLS), :] + z1[pl.ds(at, COLS), :] + z2[pl.ds(at - 1, COLS), :]
        out_ref[y] = total.astype(bf16)


def first_sum_kernel(in_ref, out_ref):
    total = in_ref[0].astype(jnp.float32)
    for k in range(1, in_ref.shape[0]):
        total = total + in_ref[k].astype(jnp.float32)
    pad = jnp.zeros((PADDED - BLOCK, CH), jnp.float32)
    for half in range(2):
        part = jnp.concatenate([total[half * BLOCK : (half + 1) * BLOCK], pad], axis=0)
        for k in range(8):
            out_ref[half * 8 + k] = part.astype(jnp.bfloat16)


def second_sum_kernel(in_ref, out_ref):
    total = in_ref[0].astype(jnp.float32)
    for k in range(1, in_ref.shape[0]):
        total = total + in_ref[k].astype(jnp.float32)
    for k in range(8):
        out_ref[k] = total


def last_kernel(in_ref, conv_ref, out_ref):
    for k in range(8):
        conv_ref[pl.ds(k * 18, 18), :] = in_ref[k, 0:18, :]
    for c in range(3):
        out_ref[c : c + 1, :] = in_ref[c, 18:19, :16]


def call(kernel, out_shape, scratch=(), smem=0, whole=0, n_in=1, flops=0, vmem=4):
    specs = [pl.BlockSpec(memory_space=pltpu.SMEM)] * smem
    specs += [pl.BlockSpec(memory_space=pltpu.HBM)] * whole
    specs += [pl.BlockSpec(memory_space=VMEM)] * (n_in - smem - whole)
    many = isinstance(out_shape, tuple)
    return pl.pallas_call(
        kernel,
        out_shape=out_shape,
        in_specs=specs,
        out_specs=tuple(pl.BlockSpec(memory_space=VMEM) for _ in out_shape)
        if many
        else pl.BlockSpec(memory_space=VMEM),
        scratch_shapes=list(scratch),
        cost_estimate=pl.CostEstimate(flops=flops, bytes_accessed=1 << 20, transcendentals=0),
        compiler_params=pltpu.CompilerParams(vmem_limit_bytes=vmem << 20),
    )


def shape(*dims, dtype=jnp.float32):
    return jax.ShapeDtypeStruct(dims, dtype)


def pack(tile, features, targets):
    out = shape(SLAB + 32, CH, dtype=jnp.bfloat16)
    return call(
        pack_kernel,
        (out, out),
        scratch=[VMEM((3, ROWS_LOC, COLS), jnp.float32), pltpu.SemaphoreType.DMA((3,))],
        smem=1,
        n_in=3,
        whole=2,
    )(
        tile,
        pltpu.with_memory_space_constraint(features, pltpu.HBM),
        pltpu.with_memory_space_constraint(targets, pltpu.HBM),
    )


def prepare(conv_weight, disc_weight, disc_head, lpips_weight, lpips_lin, out_weight):
    bf16 = jnp.bfloat16
    return call(
        prep_kernel,
        (
            shape(N_LOSS * CH, K_BAND, dtype=bf16),
            shape(3 * N_GRAD * 8, N_LOSS * CH, dtype=bf16),
            shape(CH, CH),
            shape(8, CH),
            shape(3, 4 * CH, 2 * CH, dtype=bf16),
        ),
        scratch=[VMEM((32, CH), jnp.float32)],
        n_in=6,
        flops=1 << 28,
    )(
        disc_weight, lpips_weight, disc_head.reshape(1, -1), lpips_lin.reshape(1, -1),
        out_weight.T, conv_weight,
    )


def tile_step(tile, far, own, truth, near, band, band_t, heads, out_w, two):
    f32, bf16 = jnp.float32, jnp.bfloat16
    rows = N_PRE * PITCH + 8
    return call(
        main_kernel,
        (
            shape(3, ROWS_LOC, COLS),
            shape(ROWS_LOC, COLS, CH, dtype=bf16),
            shape(COLS, CH, dtype=bf16),
            shape(COLS, CH, dtype=bf16),
            shape(32 * 2 * BLOCK, CH, dtype=bf16),
        ),
        scratch=[
            VMEM((rows, CH), f32),
            VMEM((rows, CH), f32),
            VMEM((rows, CH), f32),
            VMEM((N_GRAD, COLS, CH), f32),
            VMEM((ROWS_LOC, COLS, CH), bf16),
            VMEM((N_PRE * 8, COLS), f32),
            VMEM((N_LOSS * CH, COLS), bf16),
            VMEM((32 * 2 * BLOCK, CH), f32),
            VMEM((SLAB + 32, CH), bf16),
            VMEM((SLAB + 32, CH), bf16),
        ],
        smem=1,
        n_in=10,
        flops=1 << 31,
        vmem=20,
    )(tile, far, own, truth, near, two, out_w, band, band_t, heads)


def back_step(tile, grad_pre, far, near, conv_weight, recon):
    rows = ROWS_LOC * PITCH + 8
    return call(
        back_kernel,
        (shape(ROWS_LOC, COLS, CH, dtype=jnp.bfloat16), shape(3, ROWS_LOC, COLS)),
        scratch=[VMEM((rows, CH), jnp.float32)] * 3
        + [VMEM((ROWS_LOC + 2, COLS, CH), jnp.bfloat16)],
        smem=1,
        n_in=6,
        flops=1 << 30,
        vmem=8,
    )(tile, grad_pre, far, near, conv_weight, recon)


def swap(array, axes):
    return lax.all_to_all(array, axes, split_axis=0, concat_axis=0, tiled=True)


def swaps(firsts):
    return [pair for i in firsts for pair in ((i, i + 1), (i + 1, i))]


ROWS = ("zl", "x", "core")


def body(
    features, conv_weight, out_weight, targets, disc_weight, disc_head, lpips_weight, lpips_lin
):
    tile = lax.axis_index(ROWS).astype(jnp.int32).reshape(1)
    own, truth = features[0].reshape(TILE, CH), jnp.transpose(targets[0], (2, 0, 1))
    on_chip, off_chip = swaps(range(0, TILES, 2)), swaps(range(1, TILES - 1, 2))
    near, far = pack(tile, own, truth)
    near, far = lax.ppermute(near, ROWS, on_chip), lax.ppermute(far, ROWS, off_chip)
    tables = prepare(
        conv_weight, disc_weight, disc_head, lpips_weight, lpips_lin, out_weight
    )
    recon, grad_pre, near, far, pieces = tile_step(tile, far, own, truth, near, *tables)
    pieces = swap(pieces.reshape(32, 2 * BLOCK, CH), ("x", "core", "y"))
    pieces = call(first_sum_kernel, shape(16, PADDED, CH, dtype=jnp.bfloat16))(pieces)
    pieces, near, far = lax.optimization_barrier((pieces, near, far))
    pieces = swap(pieces, ("zh", "zl"))
    near, far = lax.ppermute(near, ROWS, on_chip), lax.ppermute(far, ROWS, off_chip)
    grad_features, recon = back_step(tile, grad_pre, far, near, conv_weight, recon)
    pieces, grad_features, recon = lax.optimization_barrier((pieces, grad_features, recon))
    pieces = call(second_sum_kernel, shape(8, PADDED, CH))(pieces)
    pieces = swap(pieces, ("x", "core"))
    grad_conv, grad_out = call(last_kernel, (shape(144, CH), shape(3, 16)))(pieces)
    return (
        jnp.transpose(recon, (1, 2, 0))[None],
        grad_features[None],
        jnp.transpose(grad_conv.reshape(3, 3, 16, CH), (0, 1, 3, 2)),
        grad_out.T,
    )


def solution(mesh):
    fine = Mesh(mesh.devices.reshape(4, 2, 8, 4, 2), ("y", "zh", "zl", "x", "core"))
    dp = ("y", "zh")
    in_specs = (
        P(dp, ROWS, None, None), P(), P(), P(dp, ROWS, None, None), P(), P(), P(), P(),
    )
    out_specs = (
        P(dp, ROWS, None, None), P(dp, ROWS, None, None), P(None, None, None, dp), P(dp, None),
    )
    return jax.shard_map(body, mesh=fine, in_specs=in_specs, out_specs=out_specs, check_vma=False)
```
